32 devices in a mesh: member: 2 (over x), lateral: 8 (over z, y), radial: 2 (over core).
Axes of the slice: x: 2, y: 2, z: 4, core: 2. Of those that a mesh axis runs over, the one named last changes fastest.
Arguments:
- initial_displacement: float32 [6, 8, 256, 2048], P('member', 'radial', 'lateral'), parts along dimension 0, may hold values from -6 to 6
- force: float32 [6, 8, 256, 2048], P('member', 'radial', 'lateral'), parts along dimension 0, may hold values from -12 to 12
- viscosity: float32 [32], P('member'), parts along dimension 0, may hold values from 0.1 to 10
- layer_index: int32 [8, 256, 2048], P('radial', 'lateral'), may hold values from 0 to 15
- response: float32 [512, 1024], P(None, 'lateral'), may hold values from 0.2 to 2
- ocean_mask: int32 [256, 2048], P('lateral'), may hold values 0 or 1
Outputs:
- displacement: float32 [6, 8, 256, 2048], P('member', 'radial', 'lateral'), parts along dimension 0
- coefficients: float32 [1024, 1024], P('member', ('lateral', 'radial')), parts along dimension 0
- sea_load: float32 [256, 4096], P('lateral', 'member'), parts along dimension 1
The draws below stay inside these ranges and needn't reach their ends.
There are 2 independent parts, one for each index of `member`. The reference program is written for one: setup_inputs(seed, part) draws one part's arguments, and reference() takes and returns one part's arrays. A program takes and returns all parts, laid end to end along the dimension named above; an argument that names none is the same for every part. Nothing has to cross between parts.
All inputs are finite; a program needn't handle non-finite values. No bound on the sum of `ocean_mask` on one device may be relied on, other than what follows from the above.
Results may differ from the reference program's by a relative error of at most 0.000073.
Values sent between devices are 32-bit elements; how exact they have to be, the bound alone decides.
A program may use at most 128 MiB of HBM per device.

```python
import math
import jax
import jax.numpy as jnp
from jax import lax

SHELLS = 8
NLON = 2048
MODES = 512
LAYERS = 16
SWEEPS = 2
NLAT = 256


def with_ends(values, own_key, low, top_value):
    dims = values.shape
    spot = [jax.random.randint(jax.random.fold_in(own_key, axis), (), 0, dims[axis]) for axis in range(len(dims))]
    values = values.at[tuple(spot)].set(low)
    longest = dims.index(max(dims))
    spot[longest] = (spot[longest] + 1) % dims[longest]
    return values.at[tuple(spot)].set(top_value)


def levels(stream_key, shape, cuts, least, largest):
    factor_of, own = 1.0, jax.random.fold_in(stream_key, 6)
    for position, shards_of in cuts:
        draws = jnp.exp(jax.random.uniform(jax.random.fold_in(own, position), (shards_of,), jnp.float32, least / len(cuts), largest / len(cuts)))
        factor_of = factor_of * jnp.repeat(draws, shape[position] // shards_of).reshape([-1 if axis == position else 1 for axis in range(len(shape))])
    return factor_of


def noise(key, dims, deviation, limit, split=(), kind=jnp.bfloat16):
    loudness = levels(key, dims, split, -0.22, 0.18) if split else 1.0
    values = jax.random.normal(key, dims, jnp.float32) * deviation * loudness
    return jnp.minimum(jnp.maximum(values, -limit), limit).astype(kind)


def setup_inputs(seed: int = 0, part: int = 0) -> dict:
    seeds = jax.random.split(jax.random.key(seed), 7)
    own_keys = jax.random.split(jax.random.fold_in(seeds[6], part), 7)
    initial_displacement = noise(own_keys[0], (3, SHELLS, NLAT, NLON), 1.0, 6.0, ((1, 2), (2, 8)), jnp.float32)
    force = noise(own_keys[1], (3, SHELLS, NLAT, NLON), 2.0, 12.0, ((1, 2), (2, 8)), jnp.float32)
    viscosity = jnp.clip(jnp.exp(jax.random.uniform(own_keys[2], (LAYERS,), jnp.float32, math.log(0.1), math.log(10.0))), 0.1, 10.0)
    layer_index = with_ends(jax.random.randint(seeds[3], (SHELLS, NLAT, NLON), 0, LAYERS), jax.random.fold_in(seeds[3], 1), 0, LAYERS - 1).astype(jnp.int32)
    response = jnp.clip(jnp.exp(math.log(2.0) - 2.3025851 * jax.random.uniform(seeds[4], (MODES, 2 * MODES), jnp.float32) ** levels(seeds[4], (MODES, 2 * MODES), ((1, 8),), -0.2, 0.2)), 0.2, 2.0)
    ocean_mask = with_ends((jax.random.randint(seeds[5], (NLAT, NLON), 0, 10) < 7).astype(jnp.int32), jax.random.fold_in(seeds[5], 1), 0, 1)
    return dict(initial_displacement=initial_displacement, force=force, viscosity=viscosity, layer_index=layer_index, response=response, ocean_mask=ocean_mask)


highest = lax.Precision.HIGHEST
relaxation = 0.8

def layer_lookup(layer_index, viscosity):
    result = jnp.zeros(layer_index.shape, jnp.float32)
    for layer_number in range(viscosity.shape[0]):
        result = result + jnp.where(layer_index == layer_number, viscosity[layer_number], jnp.zeros((), viscosity.dtype))
    return result

def longitude_table(count, columns, modes):
    points = jnp.arange(count, dtype=jnp.int32)[:, None]
    orders = (columns % modes)[None, :]
    phase = points * orders % count
    angle = 2.0 * math.pi / count * phase.astype(jnp.float32)
    table = jnp.where(columns[None, :] >= modes, jnp.sin(angle), jnp.cos(angle))
    return table * math.sqrt(2.0 / count)

def colatitude_table(count, modes):
    points = jnp.arange(count, dtype=jnp.int32)[:, None]
    waves = jnp.arange(modes, dtype=jnp.int32)[None, :]
    phase = waves * (2 * points + 1) % (4 * count)
    angle = math.pi / (2 * count) * phase.astype(jnp.float32)
    return jnp.cos(angle) * math.sqrt(2.0 / count)

def sweep(padded, eta_padded, force):
    eta_mid = eta_padded[1:-1, 1:-1]
    middle = padded[:, 1:-1, 1:-1]
    beside_eta = [eta_padded[2:, 1:-1], eta_padded[:-2, 1:-1], eta_padded[1:-1, 2:], eta_padded[1:-1, :-2], jnp.roll(eta_mid, 1, axis=-1), jnp.roll(eta_mid, -1, axis=-1)]
    beside_field = [padded[:, 2:, 1:-1], padded[:, :-2, 1:-1], padded[:, 1:-1, 2:], padded[:, 1:-1, :-2], jnp.roll(middle, 1, axis=-1), jnp.roll(middle, -1, axis=-1)]
    diagonal = jnp.ones(eta_mid.shape, eta_mid.dtype)
    pulled = jnp.zeros(middle.shape, middle.dtype)
    for other_eta, other_field in zip(beside_eta, beside_field):
        weight = 0.5 * (eta_mid + other_eta)
        diagonal = diagonal + weight
        pulled = pulled + weight[None] * other_field
    remainder = force - (diagonal[None] * middle - pulled)
    return middle + relaxation * remainder / diagonal[None]

def reference(initial_displacement, force, viscosity, layer_index, response, ocean_mask):
    eta = layer_lookup(layer_index, viscosity)
    eta_padded = jnp.pad(eta, ((1, 1), (1, 1), (0, 0)))
    displacement = initial_displacement
    for sweep_number in range(SWEEPS):
        padded = jnp.pad(displacement, ((0, 0), (1, 1), (1, 1), (0, 0)))
        displacement = sweep(padded, eta_padded, force)
    surface = displacement[0, SHELLS - 1]
    columns = jnp.arange(2 * MODES, dtype=jnp.int32)
    longitude = longitude_table(NLON, columns, MODES)
    colatitude = colatitude_table(NLAT, MODES)
    fourier = jnp.dot(surface, longitude, precision=highest)
    coefficients = jnp.dot(colatitude.T, fourier, precision=highest)
    load_spectrum = response * coefficients
    load_rows = jnp.dot(colatitude, load_spectrum, precision=highest)
    sea_load = ocean_mask.astype(jnp.float32) * jnp.dot(load_rows, longitude.T, precision=highest)
    return (displacement, coefficients, sea_load)
```

```python
import functools
import math

import jax
import jax.numpy as jnp
import ml_dtypes
import numpy as np
from jax import lax
from jax.experimental import pallas as pl
from jax.experimental.pallas import tpu as pltpu
from jax.sharding import PartitionSpec as P

MODES = 512
PAD = 8
VMEM = 67043328
MESH = pl.DeviceIdType.MESH
f32, bf16 = jnp.float32, jnp.bfloat16


def halves(table):
    table = table.astype(np.float32)
    high = table.astype(ml_dtypes.bfloat16)
    low = (table - high.astype(np.float32)).astype(ml_dtypes.bfloat16)
    return high, low


def longitude_quarter(count, modes):
    points = np.arange(count // 4)[:, None]
    phase = points * np.arange(modes)[None, :] % count
    angle = 2.0 * math.pi / count * phase
    table = np.concatenate([np.cos(angle), np.sin(angle)], axis=1)
    return halves(table * math.sqrt(2.0 / count))


def colatitude_table(count, modes):
    points = np.arange(count)[:, None]
    phase = np.arange(modes)[None, :] * (2 * points + 1) % (4 * count)
    table = np.cos(math.pi / (2 * count) * phase) * math.sqrt(2.0 / count)
    return halves(table)


def split(x):
    high = x.astype(bf16)
    return high, (x - high.astype(f32)).astype(bf16)


def dot(a, b, dims=(((1,), (0,)), ((), ()))):
    return lax.dot_general(a, b, dims, preferred_element_type=f32)


def choose(index, values):
    bit = 0
    while len(values) > 1:
        odd = (index & (1 << bit)) != 0
        values = [
            jnp.where(odd, values[min(i + 1, len(values) - 1)], values[i])
            for i in range(0, len(values), 2)
        ]
        bit += 1
    return values[0]


def kernel(lat, rad, layers, disp, force, visc, layer, response, mask, th, tl, ch, cl,
           out, coef_out, gather, th_v, tl_v, mask_v,
           u0, u1, fv, fh, li, he, fsend, frecv, gsend, grecv, resp_v, resp_t, ch_v, cl_v, visc_s,
           load_sem, x_send, x_recv, r_send, r_recv, a_send, a_recv, b_send, b_recv, far_sem):
    comps, shells, rows, lon = disp.shape
    width = response.shape[1]
    me = lax.axis_index("lateral")
    place = lax.axis_index("radial")
    inner = pl.ds(PAD, rows)
    last = shells - 1
    top = place == rad - 1
    south, north = me < lat - 1, me > 0
    face = jnp.where(top, 0, last)

    def order(i):
        return jnp.where(top, last - i, i)

    def load(source, target, index):
        copy = pltpu.make_async_copy(source, target, load_sem.at[index])
        copy.start()
        return copy

    def field(c):
        return u0.at[c, pl.ds(1, shells), inner]

    def around(d, e):
        return {"lateral": lax.rem(me + d, lat), "radial": lax.rem(place + e, rad)}

    offsets = [(d, e) for d in range(lat) for e in range(rad) if d or e]
    barrier = pltpu.get_barrier_semaphore()
    for e in range(1, rad):
        pl.semaphore_signal(barrier, inc=1, device_id=around(0, e), device_id_type=MESH)

    def greet(sem, step):
        @pl.when(me + step < lat)
        def _():
            pl.semaphore_signal(sem, inc=1, device_id={"lateral": me + step}, device_id_type=MESH)

        @pl.when(me >= step)
        def _():
            pl.semaphore_signal(sem, inc=1, device_id={"lateral": me - step}, device_id_type=MESH)

    def greeted(step):
        return jnp.where(me + step < lat, 1, 0) + jnp.where(me >= step, 1, 0)

    greet(barrier, 1)
    steps = [1 << k for k in range((lat - 1).bit_length())]

    c_visc = load(visc, visc_s, 0)
    c_layer = load(layer, li.at[pl.ds(1, shells), inner], 1)
    c_disp, c_force = [], []
    for c in range(comps):
        c_disp.append(load(disp.at[c], field(c), 2 + 2 * c))
        c_force.append(load(force.at[c], fv.at[c], 3 + 2 * c))

    void = jnp.where(top, shells + 1, 0)
    tall, wide = rows + 2 * PAD, (1, lon)
    he[void] = jnp.zeros((tall, lon), f32)
    for c in range(comps):
        u0[c, void] = jnp.zeros((tall, lon), f32)
        u1[c, void] = jnp.zeros((tall, lon), f32)

    def unpadded(row):
        for s in range(1, shells + 1):
            he[s, row:row + 1, :] = jnp.zeros(wide, f32)
            for c in range(comps):
                u0[c, s, row:row + 1, :] = jnp.zeros(wide, f32)
                u1[c, s, row:row + 1, :] = jnp.zeros(wide, f32)

    @pl.when(jnp.logical_not(north))
    def _():
        unpadded(PAD - 1)

    @pl.when(jnp.logical_not(south))
    def _():
        unpadded(PAD + rows)

    sides = [
        (0, south, north, jnp.where(south, me + 1, me), pl.ds(rows - 1, 1), pl.ds(rows - 2, 2),
         pl.ds(PAD - 1, 1), pl.ds(PAD - 2, 2), pl.ds(PAD + rows - 1, 1)),
        (1, north, south, jnp.where(north, me - 1, me), pl.ds(0, 1), pl.ds(0, 2),
         pl.ds(PAD + rows, 1), pl.ds(PAD + rows, 2), pl.ds(PAD, 1)),
    ]

    def lateral(side, k, source, target):
        return pltpu.make_async_remote_copy(
            src_ref=source, dst_ref=target, send_sem=x_send.at[side[0], k], recv_sem=x_recv.at[side[0], k],
            device_id={"lateral": side[3]}, device_id_type=MESH)

    def first(side):
        _, _, _, _, one, two, edge, pair, _ = side
        refs = [
            (disp.at[0, last, two], u0.at[0, shells, pair]),
            (layer.at[last, two], li.at[shells, pair]),
            (disp.at[0, last - 1, one], u0.at[0, shells - 1, edge]),
            (layer.at[last - 1, one], li.at[shells - 1, edge]),
            (force.at[0, last, one], fh.at[side[0]]),
        ]
        return [lateral(side, k, a, b) for k, (a, b) in enumerate(refs)]

    rest = pl.ds(1, comps - 1)

    def bulk_rest(side, i):
        s = order(i)
        return [lateral(side, 5 + i, disp.at[rest, s, side[4]], u0.at[rest, s + 1, side[6]])]

    def bulk_all(side, i):
        s = order(i)
        return [lateral(side, 5 + shells + i, layer.at[s, side[4]], li.at[s + 1, side[6]]),
                lateral(side, 5 + i, disp.at[:, s, side[4]], u0.at[:, s + 1, side[6]])]

    def later_rest(side, i):
        s = order(i)
        return [lateral(side, 5 + 2 * shells + i, u1.at[rest, s + 1, side[8]], u1.at[rest, s + 1, side[6]])]

    def later_all(side, i):
        s = order(i)
        return [lateral(side, 5 + 2 * shells + i, u1.at[:, s + 1, side[8]], u1.at[:, s + 1, side[6]])]

    def for_shell(i, act, some, every):
        alone = jnp.logical_and(top, i < some[1])

        @pl.when(alone)
        def _():
            act(some[0])

        @pl.when(jnp.logical_not(alone))
        def _():
            act(every)

    def start_to(i, some, every):
        for side in sides:
            @pl.when(side[1])
            def _():
                for_shell(i, lambda make: [c.start() for c in make(side, i)], some, every)

    def sent_to(i, some, every):
        for side in sides:
            @pl.when(side[1])
            def _():
                for_shell(i, lambda make: [c.wait_send() for c in make(side, i)], some, every)

    def got_from(i, some, every):
        for side in sides:
            @pl.when(side[2])
            def _():
                for_shell(i, lambda make: [c.wait_recv() for c in make(side, i)], some, every)

    bulk = ((bulk_rest, 2), bulk_all)
    later = ((later_rest, 1), later_all)

    def across(k, source, target):
        return pltpu.make_async_remote_copy(
            src_ref=source, dst_ref=target, send_sem=r_send.at[k], recv_sem=r_recv.at[k],
            device_id={"radial": rad - 1 - place}, device_id_type=MESH)

    beyond = jnp.where(top, shells + 1, 0)
    facing = jnp.where(top, 0, shells + 1)
    r_layer = across(0, layer.at[face], li.at[beyond, inner])
    r_disp = across(1, disp.at[:, face], u0.at[:, beyond, inner])
    r_later = across(2, u1.at[:, face + 1, inner], u1.at[:, beyond, inner])

    pl.semaphore_wait(barrier, greeted(1) + rad - 1)

    @pl.when(top)
    def _():
        for side in sides:
            @pl.when(side[1])
            def _():
                for copy in first(side):
                    copy.start()

    r_layer.start()
    r_disp.start()
    greet(far_sem.at[0], steps[0])

    @pl.when(top)
    def _():
        for i in range(shells):
            start_to(i, *bulk)

    c_visc.wait()
    values = [visc_s[i] * 0.5 for i in range(layers)]

    def lookup_at(s, where):
        he[s, where, :] = choose(li[s, where, :], values)

    def lookup(s):
        for r in range(0, rows, 8):
            lookup_at(s, pl.ds(PAD + r, 8))

    def lookup_step(i, carry):
        lookup(order(i) + 1)
        return carry

    c_layer.wait()
    lax.fori_loop(0, shells, lookup_step, 0)

    @pl.when(jnp.logical_not(top))
    def _():
        for i in range(shells):
            start_to(i, *bulk)

    tables = [(th, th_v), (tl, tl_v), (response, resp_v), (ch, ch_v), (cl, cl_v), (mask, mask_v)]
    for copy in c_disp + c_force:
        copy.wait()
    c_tables = [load(a, b, 2 + 2 * comps + k) for k, (a, b) in enumerate(tables)]

    for k, step in enumerate(steps):
        if k:
            pl.semaphore_wait(far_sem.at[k - 1], greeted(steps[k - 1]))
            greet(far_sem.at[k], step)
            break

    chunk = lon // 4

    def beside(load, k):
        first, end = k * chunk, (k + 1) * chunk
        mid = load(slice(first, end))
        before = load(slice((first - 128) % lon, (first - 128) % lon + 128))
        after = load(slice(end % lon, end % lon + 128))
        left = pltpu.roll(jnp.concatenate([before, mid], axis=1), 1, 1)[:, 128:]
        right = pltpu.roll(jnp.concatenate([mid, after], axis=1), chunk + 127, 1)[:, :chunk]
        return mid, left, right

    def sweep(src, s, r, size, some, pushed, store):
        here, next_row, last_row = slice(r, r + size), slice(r + 1, r + size + 1), slice(r - 1, r + size - 1)
        for k in range(4):
            lanes = slice(k * chunk, (k + 1) * chunk)
            h, left, right = beside(lambda cols: he[s + 1, here, cols], k)
            ws = [
                h + he[s + 2, here, lanes],
                h + he[s, here, lanes],
                h + he[s + 1, next_row, lanes],
                h + he[s + 1, last_row, lanes],
                h + left,
                h + right,
            ]
            rate = 0.8 / (1.0 + (((ws[0] + ws[1]) + (ws[2] + ws[3])) + (ws[4] + ws[5])))
            for c in some:
                u, left, right = beside(lambda cols: src[c, s + 1, here, cols], k)
                total = pushed(c, lanes)
                total = total + ws[0] * src[c, s + 2, here, lanes]
                total = total + ws[1] * src[c, s, here, lanes]
                total = total + ws[2] * src[c, s + 1, next_row, lanes]
                total = total + ws[3] * src[c, s + 1, last_row, lanes]
                total = total + ws[4] * left
                total = total + ws[5] * right
                store(c, lanes, 0.2 * u + rate * total)

    def sweep1(s, r, some):
        def store(c, lanes, value):
            u1[c, s + 1, PAD + r:PAD + r + 8, lanes] = value

        sweep(u0, s, PAD + r, 8, some, lambda c, lanes: fv[c, s, r:r + 8, lanes], store)

    def sweep2(s, r, some):
        def store(c, lanes, value):
            out[c, s, r:r + 8, lanes] = value

        sweep(u1, s, PAD + r, 8, some, lambda c, lanes: fv[c, s, r:r + 8, lanes], store)

    edge_rows = sorted({0, rows - 8})
    inner_rows = list(range(8, rows - 8, 8))
    all_comps, rest_comps = list(range(comps)), list(range(1, comps))

    def inner1(i, carry):
        s = order(i)
        for r in inner_rows:
            sweep1(s, r, all_comps)
        return carry

    lax.fori_loop(0, jnp.where(top, 2, 3), inner1, 0)

    quarter = lon // 4
    modes = th.shape[1] // 2
    wave = lax.broadcasted_iota(jnp.int32, (rows, modes), 1) & 3
    zero, one = jnp.zeros((rows, modes), f32), jnp.ones((rows, modes), f32)
    e1 = jnp.where(wave == 0, one, jnp.where(wave == 2, -one, zero))
    s1 = jnp.where(wave == 1, one, jnp.where(wave == 3, -one, zero))
    e2 = jnp.where((wave & 1) == 0, one, -one)
    half = width // rad
    forward = []
    for d, e in [(d, e) for d in range(lat) for e in range(rad) if d or e != rad - 1]:
        peer = lax.rem(me + d, lat)
        forward.append((d, e, pltpu.make_async_remote_copy(
            src_ref=fsend.at[peer, e], dst_ref=frecv.at[me],
            send_sem=a_send.at[d * rad + e], recv_sem=a_recv.at[d],
            device_id={"lateral": peer, "radial": e}, device_id_type=MESH)))

    @pl.when(top)
    def _():
        for side in sides:
            @pl.when(side[2])
            def _():
                for copy in first(side):
                    copy.wait_recv()
                lookup_at(shells, side[7])
                lookup_at(shells - 1, side[6])

        def early(i, carry):
            for r in edge_rows:
                sweep1(last - i, r, [0])
            return carry

        lax.fori_loop(0, 2, early, 0)
        for side, row in zip(sides, (PAD - 1, PAD + rows)):
            @pl.when(side[2])
            def _():
                def store(c, lanes, value):
                    u1[c, shells, row:row + 1, lanes] = value

                sweep(u0, last, row, 1, [0], lambda c, lanes: fh[side[0], :, lanes], store)

        for r in range(0, rows, 8):
            sweep2(last, r, [0])

    for copy in c_tables[:2]:
        copy.wait()

    @pl.when(top)
    def _():
        x = jnp.concatenate([out[0, last, :, quarter * m:quarter * (m + 1)] for m in range(4)], axis=0)
        xh, xl = split(x)
        g = dot(xh, th_v[...]) + dot(xl, th_v[...]) + dot(xh, tl_v[...])
        gc = [g[rows * m:rows * (m + 1), :modes] for m in range(4)]
        gs = [g[rows * m:rows * (m + 1), modes:] for m in range(4)]
        fc = gc[0] + e2 * gc[2] + e1 * (gc[1] + gc[3]) - s1 * (gs[1] - gs[3])
        fs = gs[0] + e2 * gs[2] + e1 * (gs[1] + gs[3]) + s1 * (gc[1] - gc[3])
        fourier = jnp.concatenate([fc, fs], axis=1)
        for p in range(lat):
            for e in range(rad):
                fsend[p, e] = fourier[:, p * width + e * half:p * width + (e + 1) * half]

    for k, step in enumerate(steps):
        if k > 1:
            pl.semaphore_wait(far_sem.at[k - 1], greeted(steps[k - 1]))
            greet(far_sem.at[k], step)
    pl.semaphore_wait(far_sem.at[len(steps) - 1], greeted(steps[-1]))

    @pl.when(top)
    def _():
        for _, _, copy in forward:
            copy.start()
        frecv[me] = fsend[me, rad - 1]

    def main(i, carry):
        s = order(i)

        @pl.when(i == last)
        def _():
            r_layer.wait_recv()
            r_disp.wait_recv()
            lookup(facing)

        @pl.when(jnp.logical_or(jnp.logical_and(top, i == 2), i == last))
        def _():
            inner1(i, 0)

        got_from(i, *bulk)
        for side in sides:
            @pl.when(jnp.logical_and(side[2], jnp.logical_not(jnp.logical_and(top, i < 2))))
            def _():
                lookup_at(s + 1, side[6])

        for r in edge_rows:
            sweep1(s, r, all_comps)
        start_to(i, *later)
        return carry

    lax.fori_loop(0, shells, main, 0)
    r_later.start()

    def inner2(i, carry):
        s = order(i)
        alone = jnp.logical_and(top, i == 0)

        @pl.when(alone)
        def _():
            for r in inner_rows:
                sweep2(s, r, rest_comps)

        @pl.when(jnp.logical_not(alone))
        def _():
            for r in inner_rows:
                sweep2(s, r, all_comps)

        return carry

    lax.fori_loop(0, last, inner2, 0)

    for copy in c_tables[2:]:
        copy.wait()
    answer = resp_v[:, :half]
    for e in range(1, rad):
        answer = jnp.where(place == e, resp_v[:, e * half:(e + 1) * half], answer)
    resp_t[...] = answer.T

    @pl.when(top)
    def _():
        for d, e, copy in forward:
            if e == rad - 1:
                copy.wait_recv()

    @pl.when(jnp.logical_not(top))
    def _():
        for d, e, copy in forward:
            if e == 0:
                copy.wait_recv()

    spectrum = frecv[...].reshape(lat * rows, half)
    sh, sl = split(spectrum)
    down = (((0,), (0,)), ((), ()))
    both = dot(jnp.concatenate([sh, sl], axis=1), ch_v[...], down)
    coef = both[:half] + both[half:] + dot(sh, cl_v[...], down)
    sh, sl = split(resp_t[...] * coef)
    nt = (((1,), (1,)), ((), ()))
    load_rows = dot(ch_v[...], sh, nt) + dot(ch_v[...], sl, nt) + dot(cl_v[...], sh, nt)
    gsend[...] = load_rows.reshape(lat, rows, half)
    back = []
    for d, e in offsets:
        back.append(pltpu.make_async_remote_copy(
            src_ref=gsend.at[lax.rem(me + d, lat)], dst_ref=grecv.at[me, place],
            send_sem=b_send.at[d * rad + e], recv_sem=b_recv.at[d * rad + e],
            device_id=around(d, e), device_id_type=MESH))
    for copy in back:
        copy.start()
    grecv[me, place] = gsend[me]
    coef_out[...] = coef

    def final(i, carry):
        s = order(i)
        alone = jnp.logical_and(top, i == 0)

        @pl.when(i == last)
        def _():
            r_later.wait_recv()
            inner2(i, 0)

        got_from(i, *later)

        @pl.when(alone)
        def _():
            for r in edge_rows:
                sweep2(s, r, rest_comps)

        @pl.when(jnp.logical_not(alone))
        def _():
            for r in edge_rows:
                sweep2(s, r, all_comps)

        return carry

    lax.fori_loop(0, shells, final, 0)

    @pl.when(top)
    def _():
        for _, _, copy in forward:
            copy.wait_send()
        for side in sides:
            @pl.when(side[1])
            def _():
                for copy in first(side):
                    copy.wait_send()

    def settle(i, carry):
        sent_to(i, *bulk)
        sent_to(i, *later)
        return carry

    lax.fori_loop(0, shells, settle, 0)
    for copy in (r_layer, r_disp, r_later):
        copy.wait_send()
    for copy in back:
        copy.wait()
    for p in range(lat):
        for e in range(rad):
            gather[:, p * width + e * half:p * width + (e + 1) * half] = grecv[p, e]


def finish(out, coef, gather, th, tl, mask, out_h, coef_h, sea_h, sea, sem):
    rows, lon = mask.shape
    quarter, modes = lon // 4, th.shape[1] // 2
    copies = [pltpu.make_async_copy(out, out_h, sem.at[0]), pltpu.make_async_copy(coef, coef_h, sem.at[1])]
    for copy in copies:
        copy.start()
    wave = lax.broadcasted_iota(jnp.int32, (rows, modes), 1) & 3
    zero, one = jnp.zeros((rows, modes), f32), jnp.ones((rows, modes), f32)
    e1 = jnp.where(wave == 0, one, jnp.where(wave == 2, -one, zero))
    s1 = jnp.where(wave == 1, one, jnp.where(wave == 3, -one, zero))
    e2 = jnp.where((wave & 1) == 0, one, -one)
    rc, rs = gather[:, :modes], gather[:, modes:]
    twisted = [
        (rc, rs),
        (e1 * rc + s1 * rs, e1 * rs - s1 * rc),
        (e2 * rc, e2 * rs),
        (e1 * rc - s1 * rs, e1 * rs + s1 * rc),
    ]
    a = jnp.concatenate([jnp.concatenate(pair, axis=1) for pair in twisted], axis=0)
    ah, al = split(a)
    nt = (((1,), (1,)), ((), ()))
    total = dot(ah, th[...], nt) + dot(al, th[...], nt) + dot(ah, tl[...], nt)
    for m in range(4):
        cut = slice(quarter * m, quarter * (m + 1))
        sea[:, cut] = mask[:, cut].astype(f32) * total[rows * m:rows * (m + 1)]
        copies.append(pltpu.make_async_copy(sea.at[:, cut], sea_h.at[:, cut], sem.at[2 + m]))
        copies[-1].start()
    for copy in copies:
        copy.wait()


def shards(lat, rad, disp, force, visc, layer, response, mask):
    comps, shells, rows, lon = disp.shape
    width = response.shape[1]
    th, tl = longitude_quarter(lon, MODES)
    ch, cl = colatitude_table(lat * rows, MODES)
    tables = [th, tl, ch, cl]
    hbm = pl.BlockSpec(memory_space=pltpu.HBM)
    vmem = pl.BlockSpec(memory_space=pltpu.VMEM)
    tall = rows + 2 * PAD
    field = pltpu.VMEM((comps, shells + 2, tall, lon), f32)
    half = width // rad
    block = pltpu.VMEM((lat, rows, half), f32)
    dma = pltpu.SemaphoreType.DMA
    spare = 4 * (disp.size + MODES * width // rad + 2 * rows * MODES + rows * lon) + 2 * (th.size + tl.size) + 65536
    kinds = 5 + 3 * shells
    out, coef, gather, th_v, tl_v, mask_v = pl.pallas_call(
        functools.partial(kernel, lat, rad, visc.shape[0]),
        out_shape=(
            pltpu.VMEM(disp.shape, f32),
            pltpu.VMEM((width // rad, MODES), f32),
            pltpu.VMEM((rows, 2 * MODES), f32),
            pltpu.VMEM(th.shape, bf16),
            pltpu.VMEM(tl.shape, bf16),
            pltpu.VMEM(mask.shape, jnp.int32),
        ),
        in_specs=[hbm] * 10,
        out_specs=(vmem,) * 6,
        scratch_shapes=[
            field, field,
            pltpu.VMEM((comps, shells, rows, lon), f32),
            pltpu.VMEM((2, 1, lon), f32),
            pltpu.VMEM((shells + 2, tall, lon), jnp.int32),
            pltpu.VMEM((shells + 2, tall, lon), f32),
            pltpu.VMEM((lat, rad, rows, half), f32), block, block, pltpu.VMEM((lat, rad, rows, half), f32),
            pltpu.VMEM(response.shape, f32), pltpu.VMEM((half, MODES), f32),
        ] + [pltpu.VMEM(t.shape, bf16) for t in tables[2:]] + [
            pltpu.SMEM(visc.shape, f32),
            dma((2 + 2 * comps + 6,)), dma((2, kinds)), dma((2, kinds)), dma((3,)), dma((3,)),
            dma((lat * rad,)), dma((lat,)), dma((lat * rad,)), dma((lat * rad,)),
            pltpu.SemaphoreType.REGULAR((max(1, (lat - 1).bit_length()),)),
        ],
        compiler_params=pltpu.CompilerParams(
            collective_id=0, has_side_effects=True, vmem_limit_bytes=VMEM - spare),
    )(disp, force, visc, layer, response, mask, *[jnp.asarray(t) for t in tables])
    out, coef, sea = pl.pallas_call(
        finish,
        out_shape=tuple(jax.ShapeDtypeStruct(shape, f32) for shape in (out.shape, coef.shape, mask.shape)),
        in_specs=[vmem] * 6,
        out_specs=(hbm, hbm, hbm),
        scratch_shapes=[pltpu.VMEM(mask.shape, f32), dma((6,))],
        compiler_params=pltpu.CompilerParams(vmem_limit_bytes=8 << 20),
    )(out, coef, gather, th_v, tl_v, mask_v)
    return out, coef.T, sea


def solution(mesh):
    in_specs = (
        P("member", "radial", "lateral", None),
        P("member", "radial", "lateral", None),
        P("member"),
        P("radial", "lateral", None),
        P(None, "lateral"),
        P("lateral", None),
    )
    out_specs = (
        P("member", "radial", "lateral", None),
        P("member", ("lateral", "radial")),
        P("lateral", "member"),
    )
    body = functools.partial(shards, mesh.shape["lateral"], mesh.shape["radial"])
    return jax.shard_map(body, mesh=mesh, in_specs=in_specs, out_specs=out_specs, check_vma=False)
```

```python
import functools
import math

import jax
import jax.numpy as jnp
import ml_dtypes
import numpy as np
from jax import lax
from jax.experimental import pallas as pl
from jax.experimental.pallas import tpu as pltpu
from jax.sharding import PartitionSpec as P

MODES = 512
PAD = 8
VMEM = 67043328
MESH = pl.DeviceIdType.MESH
f32, bf16 = jnp.float32, jnp.bfloat16


def halves(table):
    table = table.astype(np.float32)
    high = table.astype(ml_dtypes.bfloat16)
    low = (table - high.astype(np.float32)).astype(ml_dtypes.bfloat16)
    return high, low


def longitude_quarter(count, modes):
    points = np.arange(count // 4)[:, None]
    phase = points * np.arange(modes)[None, :] % count
    angle = 2.0 * math.pi / count * phase
    table = np.concatenate([np.cos(angle), np.sin(angle)], axis=1)
    return halves(table * math.sqrt(2.0 / count))


def colatitude_table(count, modes):
    points = np.arange(count)[:, None]
    phase = np.arange(modes)[None, :] * (2 * points + 1) % (4 * count)
    table = np.cos(math.pi / (2 * count) * phase) * math.sqrt(2.0 / count)
    return halves(table)


def split(x):
    high = x.astype(bf16)
    return high, (x - high.astype(f32)).astype(bf16)


def dot(a, b, dims=(((1,), (0,)), ((), ()))):
    return lax.dot_general(a, b, dims, preferred_element_type=f32)


def choose(index, values):
    bit = 0
    while len(values) > 1:
        odd = (index & (1 << bit)) != 0
        values = [
            jnp.where(odd, values[min(i + 1, len(values) - 1)], values[i])
            for i in range(0, len(values), 2)
        ]
        bit += 1
    return values[0]


def kernel(lat, rad, layers, disp, force, visc, layer, response, mask, th, tl, ch, cl,
           out, coef_out, gather, th_v, tl_v, mask_v,
           u0, u1, fv, fh, li, he, fsend, frecv, gsend, grecv, resp_v, resp_t, ch_v, cl_v, visc_s,
           load_sem, x_send, x_recv, r_send, r_recv, a_send, a_recv, b_send, b_recv, far_sem):
    comps, shells, rows, lon = disp.shape
    width = response.shape[1]
    me = lax.axis_index("lateral")
    place = lax.axis_index("radial")
    inner = pl.ds(PAD, rows)
    last = shells - 1
    top = place == rad - 1
    south, north = me < lat - 1, me > 0
    face = jnp.where(top, 0, last)

    def order(i):
        return jnp.where(top, last - i, i)

    def load(source, target, index):
        copy = pltpu.make_async_copy(source, target, load_sem.at[index])
        copy.start()
        return copy

    def field(c):
        return u0.at[c, pl.ds(1, shells), inner]

    def around(d, e):
        return {"lateral": lax.rem(me + d, lat), "radial": lax.rem(place + e, rad)}

    offsets = [(d, e) for d in range(lat) for e in range(rad) if d or e]
    barrier = pltpu.get_barrier_semaphore()
    for e in range(1, rad):
        pl.semaphore_signal(barrier, inc=1, device_id=around(0, e), device_id_type=MESH)

    def greet(sem, step):
        @pl.when(me + step < lat)
        def _():
            pl.semaphore_signal(sem, inc=1, device_id={"lateral": me + step}, device_id_type=MESH)

        @pl.when(me >= step)
        def _():
            pl.semaphore_signal(sem, inc=1, device_id={"lateral": me - step}, device_id_type=MESH)

    def greeted(step):
        return jnp.where(me + step < lat, 1, 0) + jnp.where(me >= step, 1, 0)

    greet(barrier, 1)
    steps = [1 << k for k in range((lat - 1).bit_length())]

    c_visc = load(visc, visc_s, 0)
    c_layer = load(layer, li.at[pl.ds(1, shells), inner], 1)
    c_disp, c_force = [], []
    for c in range(comps):
        c_disp.append(load(disp.at[c], field(c), 2 + 2 * c))
        c_force.append(load(force.at[c], fv.at[c], 3 + 2 * c))

    void = jnp.where(top, shells + 1, 0)
    tall, wide = rows + 2 * PAD, (1, lon)
    he[void] = jnp.zeros((tall, lon), f32)
    for c in range(comps):
        u0[c, void] = jnp.zeros((tall, lon), f32)
        u1[c, void] = jnp.zeros((tall, lon), f32)

    def unpadded(row):
        for s in range(1, shells + 1):
            he[s, row:row + 1, :] = jnp.zeros(wide, f32)
            for c in range(comps):
                u0[c, s, row:row + 1, :] = jnp.zeros(wide, f32)
                u1[c, s, row:row + 1, :] = jnp.zeros(wide, f32)

    @pl.when(jnp.logical_not(north))
    def _():
        unpadded(PAD - 1)

    @pl.when(jnp.logical_not(south))
    def _():
        unpadded(PAD + rows)

    sides = [
        (0, south, north, jnp.where(south, me + 1, me), pl.ds(rows - 1, 1), pl.ds(rows - 2, 2),
         pl.ds(PAD - 1, 1), pl.ds(PAD - 2, 2), pl.ds(PAD + rows - 1, 1)),
        (1, north, south, jnp.where(north, me - 1, me), pl.ds(0, 1), pl.ds(0, 2),
         pl.ds(PAD + rows, 1), pl.ds(PAD + rows, 2), pl.ds(PAD, 1)),
    ]

    def lateral(side, k, source, target):
        return pltpu.make_async_remote_copy(
            src_ref=source, dst_ref=target, send_sem=x_send.at[side[0], k], recv_sem=x_recv.at[side[0], k],
            device_id={"lateral": side[3]}, device_id_type=MESH)

    def first(side):
        _, _, _, _, one, two, edge, pair, _ = side
        refs = [
            (disp.at[0, last, two], u0.at[0, shells, pair]),
            (layer.at[last, two], li.at[shells, pair]),
            (disp.at[0, last - 1, one], u0.at[0, shells - 1, edge]),
            (layer.at[last - 1, one], li.at[shells - 1, edge]),
            (force.at[0, last, one], fh.at[side[0]]),
        ]
        return [lateral(side, k, a, b) for k, (a, b) in enumerate(refs)]

    rest = pl.ds(1, comps - 1)

    def bulk_rest(side, i):
        s = order(i)
        return [lateral(side, 5 + i, disp.at[rest, s, side[4]], u0.at[rest, s + 1, side[6]])]

    def bulk_all(side, i):
        s = order(i)
        return [lateral(side, 5 + shells + i, layer.at[s, side[4]], li.at[s + 1, side[6]]),
                lateral(side, 5 + i, disp.at[:, s, side[4]], u0.at[:, s + 1, side[6]])]

    def later_rest(side, i):
        s = order(i)
        return [lateral(side, 5 + 2 * shells + i, u1.at[rest, s + 1, side[8]], u1.at[rest, s + 1, side[6]])]

    def later_all(side, i):
        s = order(i)
        return [lateral(side, 5 + 2 * shells + i, u1.at[:, s + 1, side[8]], u1.at[:, s + 1, side[6]])]

    def for_shell(i, act, some, every):
        alone = jnp.logical_and(top, i < some[1])

        @pl.when(alone)
        def _():
            act(some[0])

        @pl.when(jnp.logical_not(alone))
        def _():
            act(every)

    odd = lax.rem(me, 2) == 1

    def nearer_first(go):
        @pl.when(odd)
        def _():
            go(sides[1])

        go(sides[0])

        @pl.when(jnp.logical_not(odd))
        def _():
            go(sides[1])

    def start_to(i, some, every):
        for side in sides:
            @pl.when(side[1])
            def _():
                for_shell(i, lambda make: [c.start() for c in make(side, i)], some, every)

    def start_bulk(near):
        for side in sides:
            @pl.when(jnp.logical_and(side[1], odd == ((side[0] == 1) == near)))
            def _():
                for i in range(shells):
                    for_shell(i, lambda make: [c.start() for c in make(side, i)], *bulk)

    def sent_to(i, some, every):
        for side in sides:
            @pl.when(side[1])
            def _():
                for_shell(i, lambda make: [c.wait_send() for c in make(side, i)], some, every)

    def got_from(i, some, every):
        for side in sides:
            @pl.when(side[2])
            def _():
                for_shell(i, lambda make: [c.wait_recv() for c in make(side, i)], some, every)

    bulk = ((bulk_rest, 2), bulk_all)
    later = ((later_rest, 1), later_all)

    def across(k, source, target):
        return pltpu.make_async_remote_copy(
            src_ref=source, dst_ref=target, send_sem=r_send.at[k], recv_sem=r_recv.at[k],
            device_id={"radial": rad - 1 - place}, device_id_type=MESH)

    beyond = jnp.where(top, shells + 1, 0)
    facing = jnp.where(top, 0, shells + 1)
    r_layer = across(0, layer.at[face], li.at[beyond, inner])
    r_disp = across(1, disp.at[:, face], u0.at[:, beyond, inner])
    r_later = across(2, u1.at[:, face + 1, inner], u1.at[:, beyond, inner])

    pl.semaphore_wait(barrier, greeted(1) + rad - 1)

    @pl.when(top)
    def _():
        def go(side):
            @pl.when(side[1])
            def _():
                for copy in first(side):
                    copy.start()

        nearer_first(go)

    r_layer.start()
    r_disp.start()
    greet(far_sem.at[0], steps[0])

    c_visc.wait()
    values = [visc_s[i] * 0.5 for i in range(layers)]

    def lookup_at(s, where):
        he[s, where, :] = choose(li[s, where, :], values)

    def lookup(s):
        for r in range(0, rows, 8):
            lookup_at(s, pl.ds(PAD + r, 8))

    def lookup_step(i, carry):
        lookup(order(i) + 1)
        return carry

    c_layer.wait()
    lax.fori_loop(0, shells, lookup_step, 0)

    start_bulk(True)

    tables = [(th, th_v), (tl, tl_v), (response, resp_v), (ch, ch_v), (cl, cl_v), (mask, mask_v)]
    for copy in c_disp + c_force:
        copy.wait()
    c_tables = [load(a, b, 2 + 2 * comps + k) for k, (a, b) in enumerate(tables)]

    if steps[1:]:
        pl.semaphore_wait(far_sem.at[0], greeted(steps[0]))
        greet(far_sem.at[1], steps[1])

    chunk = lon // 4

    def beside(load, k):
        first, end = k * chunk, (k + 1) * chunk
        mid = load(slice(first, end))
        before = load(slice((first - 128) % lon, (first - 128) % lon + 128))
        after = load(slice(end % lon, end % lon + 128))
        left = pltpu.roll(jnp.concatenate([before, mid], axis=1), 1, 1)[:, 128:]
        right = pltpu.roll(jnp.concatenate([mid, after], axis=1), chunk + 127, 1)[:, :chunk]
        return mid, left, right

    def sweep(src, s, r, size, some, pushed, store):
        here, next_row, last_row = slice(r, r + size), slice(r + 1, r + size + 1), slice(r - 1, r + size - 1)
        for k in range(4):
            lanes = slice(k * chunk, (k + 1) * chunk)
            h, left, right = beside(lambda cols: he[s + 1, here, cols], k)
            ws = [
                h + he[s + 2, here, lanes],
                h + he[s, here, lanes],
                h + he[s + 1, next_row, lanes],
                h + he[s + 1, last_row, lanes],
                h + left,
                h + right,
            ]
            rate = 0.8 / (1.0 + (((ws[0] + ws[1]) + (ws[2] + ws[3])) + (ws[4] + ws[5])))
            for c in some:
                u, left, right = beside(lambda cols: src[c, s + 1, here, cols], k)
                total = pushed(c, lanes)
                total = total + ws[0] * src[c, s + 2, here, lanes]
                total = total + ws[1] * src[c, s, here, lanes]
                total = total + ws[2] * src[c, s + 1, next_row, lanes]
                total = total + ws[3] * src[c, s + 1, last_row, lanes]
                total = total + ws[4] * left
                total = total + ws[5] * right
                store(c, lanes, 0.2 * u + rate * total)

    def sweep1(s, r, some):
        def store(c, lanes, value):
            u1[c, s + 1, PAD + r:PAD + r + 8, lanes] = value

        sweep(u0, s, PAD + r, 8, some, lambda c, lanes: fv[c, s, r:r + 8, lanes], store)

    def sweep2(s, r, some):
        def store(c, lanes, value):
            out[c, s, r:r + 8, lanes] = value

        sweep(u1, s, PAD + r, 8, some, lambda c, lanes: fv[c, s, r:r + 8, lanes], store)

    edge_rows = sorted({0, rows - 8})
    inner_rows = list(range(8, rows - 8, 8))
    all_comps, rest_comps = list(range(comps)), list(range(1, comps))

    def inner1(i, carry):
        s = order(i)
        for r in inner_rows:
            sweep1(s, r, all_comps)
        return carry

    lax.fori_loop(0, jnp.where(top, 2, 3), inner1, 0)
    start_bulk(False)

    for k, step in enumerate(steps):
        if k > 1:
            pl.semaphore_wait(far_sem.at[k - 1], greeted(steps[k - 1]))
            greet(far_sem.at[k], step)

    quarter = lon // 4
    modes = th.shape[1] // 2
    wave = lax.broadcasted_iota(jnp.int32, (rows, modes), 1) & 3
    zero, one = jnp.zeros((rows, modes), f32), jnp.ones((rows, modes), f32)
    e1 = jnp.where(wave == 0, one, jnp.where(wave == 2, -one, zero))
    s1 = jnp.where(wave == 1, one, jnp.where(wave == 3, -one, zero))
    e2 = jnp.where((wave & 1) == 0, one, -one)
    half = width // rad
    forward = []
    for d, e in [(d, e) for d in range(lat) for e in range(rad) if d or e != rad - 1]:
        peer = lax.rem(me + d, lat)
        forward.append((d, e, pltpu.make_async_remote_copy(
            src_ref=fsend.at[peer, e], dst_ref=frecv.at[me],
            send_sem=a_send.at[d * rad + e], recv_sem=a_recv.at[d],
            device_id={"lateral": peer, "radial": e}, device_id_type=MESH)))

    @pl.when(top)
    def _():
        for side in sides:
            @pl.when(side[2])
            def _():
                for copy in first(side):
                    copy.wait_recv()
                lookup_at(shells, side[7])
                lookup_at(shells - 1, side[6])

        def early(i, carry):
            for r in edge_rows:
                sweep1(last - i, r, [0])
            return carry

        lax.fori_loop(0, 2, early, 0)
        for side, row in zip(sides, (PAD - 1, PAD + rows)):
            @pl.when(side[2])
            def _():
                def store(c, lanes, value):
                    u1[c, shells, row:row + 1, lanes] = value

                sweep(u0, last, row, 1, [0], lambda c, lanes: fh[side[0], :, lanes], store)

        for r in range(0, rows, 8):
            sweep2(last, r, [0])

    for copy in c_tables[:2]:
        copy.wait()

    @pl.when(top)
    def _():
        x = jnp.concatenate([out[0, last, :, quarter * m:quarter * (m + 1)] for m in range(4)], axis=0)
        xh, xl = split(x)
        g = dot(xh, th_v[...]) + dot(xl, th_v[...]) + dot(xh, tl_v[...])
        gc = [g[rows * m:rows * (m + 1), :modes] for m in range(4)]
        gs = [g[rows * m:rows * (m + 1), modes:] for m in range(4)]
        fc = gc[0] + e2 * gc[2] + e1 * (gc[1] + gc[3]) - s1 * (gs[1] - gs[3])
        fs = gs[0] + e2 * gs[2] + e1 * (gs[1] + gs[3]) + s1 * (gc[1] - gc[3])
        fourier = jnp.concatenate([fc, fs], axis=1)
        for p in range(lat):
            for e in range(rad):
                fsend[p, e] = fourier[:, p * width + e * half:p * width + (e + 1) * half]

    pl.semaphore_wait(far_sem.at[len(steps) - 1], greeted(steps[-1]))

    @pl.when(top)
    def _():
        for _, _, copy in forward:
            copy.start()
        frecv[me] = fsend[me, rad - 1]

    def main(i, carry):
        s = order(i)

        @pl.when(i == last)
        def _():
            r_layer.wait_recv()
            r_disp.wait_recv()
            lookup(facing)

        @pl.when(jnp.logical_or(jnp.logical_and(top, i == 2), i == last))
        def _():
            inner1(i, 0)

        got_from(i, *bulk)
        for side in sides:
            @pl.when(jnp.logical_and(side[2], jnp.logical_not(jnp.logical_and(top, i < 2))))
            def _():
                lookup_at(s + 1, side[6])

        for r in edge_rows:
            sweep1(s, r, all_comps)
        start_to(i, *later)
        return carry

    lax.fori_loop(0, shells, main, 0)
    r_later.start()

    def inner2(i, carry):
        s = order(i)
        alone = jnp.logical_and(top, i == 0)

        @pl.when(alone)
        def _():
            for r in inner_rows:
                sweep2(s, r, rest_comps)

        @pl.when(jnp.logical_not(alone))
        def _():
            for r in inner_rows:
                sweep2(s, r, all_comps)

        return carry

    for copy in c_tables[2:]:
        copy.wait()
    answer = resp_v[:, :half]
    for e in range(1, rad):
        answer = jnp.where(place == e, resp_v[:, e * half:(e + 1) * half], answer)
    resp_t[...] = answer.T

    @pl.when(top)
    def _():
        for d, e, copy in forward:
            if e == rad - 1:
                copy.wait_recv()

    @pl.when(jnp.logical_not(top))
    def _():
        for d, e, copy in forward:
            if e == 0:
                copy.wait_recv()

    spectrum = frecv[...].reshape(lat * rows, half)
    sh, sl = split(spectrum)
    down = (((0,), (0,)), ((), ()))
    both = dot(jnp.concatenate([sh, sl], axis=1), ch_v[...], down)
    coef = both[:half] + both[half:] + dot(sh, cl_v[...], down)
    sh, sl = split(resp_t[...] * coef)
    nt = (((1,), (1,)), ((), ()))
    load_rows = dot(ch_v[...], sh, nt) + dot(ch_v[...], sl, nt) + dot(cl_v[...], sh, nt)
    gsend[...] = load_rows.reshape(lat, rows, half)
    back = []
    for d, e in offsets:
        back.append(pltpu.make_async_remote_copy(
            src_ref=gsend.at[lax.rem(me + d, lat)], dst_ref=grecv.at[me, place],
            send_sem=b_send.at[d * rad + e], recv_sem=b_recv.at[d * rad + e],
            device_id=around(d, e), device_id_type=MESH))
    for copy in back:
        copy.start()
    grecv[me, place] = gsend[me]
    coef_out[...] = coef

    def final(i, carry):
        s = order(i)
        alone = jnp.logical_and(top, i == 0)

        @pl.when(i == last)
        def _():
            r_later.wait_recv()
            inner2(i, 0)

        got_from(i, *later)

        @pl.when(alone)
        def _():
            for r in edge_rows:
                sweep2(s, r, rest_comps)

        @pl.when(jnp.logical_not(alone))
        def _():
            for r in edge_rows:
                sweep2(s, r, all_comps)

        return carry

    lax.fori_loop(0, last, inner2, 0)

    lax.fori_loop(0, shells, final, 0)

    @pl.when(top)
    def _():
        for _, _, copy in forward:
            copy.wait_send()
        for side in sides:
            @pl.when(side[1])
            def _():
                for copy in first(side):
                    copy.wait_send()

    def settle(i, carry):
        sent_to(i, *bulk)
        sent_to(i, *later)
        return carry

    lax.fori_loop(0, shells, settle, 0)
    for copy in (r_layer, r_disp, r_later):
        copy.wait_send()
    for copy in back:
        copy.wait()
    for p in range(lat):
        for e in range(rad):
            gather[:, p * width + e * half:p * width + (e + 1) * half] = grecv[p, e]


def finish(out, coef, gather, th, tl, mask, out_h, coef_h, sea_h, sea, sem):
    rows, lon = mask.shape
    quarter, modes = lon // 4, th.shape[1] // 2
    copies = [pltpu.make_async_copy(out, out_h, sem.at[0]), pltpu.make_async_copy(coef, coef_h, sem.at[1])]
    for copy in copies:
        copy.start()
    wave = lax.broadcasted_iota(jnp.int32, (rows, modes), 1) & 3
    zero, one = jnp.zeros((rows, modes), f32), jnp.ones((rows, modes), f32)
    e1 = jnp.where(wave == 0, one, jnp.where(wave == 2, -one, zero))
    s1 = jnp.where(wave == 1, one, jnp.where(wave == 3, -one, zero))
    e2 = jnp.where((wave & 1) == 0, one, -one)
    rc, rs = gather[:, :modes], gather[:, modes:]
    twisted = [
        (rc, rs),
        (e1 * rc + s1 * rs, e1 * rs - s1 * rc),
        (e2 * rc, e2 * rs),
        (e1 * rc - s1 * rs, e1 * rs + s1 * rc),
    ]
    a = jnp.concatenate([jnp.concatenate(pair, axis=1) for pair in twisted], axis=0)
    ah, al = split(a)
    nt = (((1,), (1,)), ((), ()))
    total = dot(ah, th[...], nt) + dot(al, th[...], nt) + dot(ah, tl[...], nt)
    for m in range(4):
        cut = slice(quarter * m, quarter * (m + 1))
        sea[:, cut] = mask[:, cut].astype(f32) * total[rows * m:rows * (m + 1)]
        copies.append(pltpu.make_async_copy(sea.at[:, cut], sea_h.at[:, cut], sem.at[2 + m]))
        copies[-1].start()
    for copy in copies:
        copy.wait()


def shards(lat, rad, disp, force, visc, layer, response, mask):
    comps, shells, rows, lon = disp.shape
    width = response.shape[1]
    th, tl = longitude_quarter(lon, MODES)
    ch, cl = colatitude_table(lat * rows, MODES)
    tables = [th, tl, ch, cl]
    hbm = pl.BlockSpec(memory_space=pltpu.HBM)
    vmem = pl.BlockSpec(memory_space=pltpu.VMEM)
    tall = rows + 2 * PAD
    field = pltpu.VMEM((comps, shells + 2, tall, lon), f32)
    half = width // rad
    block = pltpu.VMEM((lat, rows, half), f32)
    dma = pltpu.SemaphoreType.DMA
    spare = 4 * (disp.size + MODES * width // rad + 2 * rows * MODES + rows * lon) + 2 * (th.size + tl.size) + 65536
    kinds = 5 + 3 * shells
    out, coef, gather, th_v, tl_v, mask_v = pl.pallas_call(
        functools.partial(kernel, lat, rad, visc.shape[0]),
        out_shape=(
            pltpu.VMEM(disp.shape, f32),
            pltpu.VMEM((width // rad, MODES), f32),
            pltpu.VMEM((rows, 2 * MODES), f32),
            pltpu.VMEM(th.shape, bf16),
            pltpu.VMEM(tl.shape, bf16),
            pltpu.VMEM(mask.shape, jnp.int32),
        ),
        in_specs=[hbm] * 10,
        out_specs=(vmem,) * 6,
        scratch_shapes=[
            field, field,
            pltpu.VMEM((comps, shells, rows, lon), f32),
            pltpu.VMEM((2, 1, lon), f32),
            pltpu.VMEM((shells + 2, tall, lon), jnp.int32),
            pltpu.VMEM((shells + 2, tall, lon), f32),
            pltpu.VMEM((lat, rad, rows, half), f32), block, block, pltpu.VMEM((lat, rad, rows, half), f32),
            pltpu.VMEM(response.shape, f32), pltpu.VMEM((half, MODES), f32),
        ] + [pltpu.VMEM(t.shape, bf16) for t in tables[2:]] + [
            pltpu.SMEM(visc.shape, f32),
            dma((2 + 2 * comps + 6,)), dma((2, kinds)), dma((2, kinds)), dma((3,)), dma((3,)),
            dma((lat * rad,)), dma((lat,)), dma((lat * rad,)), dma((lat * rad,)),
            pltpu.SemaphoreType.REGULAR((max(1, (lat - 1).bit_length()),)),
        ],
        compiler_params=pltpu.CompilerParams(
            collective_id=0, has_side_effects=True, vmem_limit_bytes=VMEM - spare),
    )(disp, force, visc, layer, response, mask, *[jnp.asarray(t) for t in tables])
    out, coef, sea = pl.pallas_call(
        finish,
        out_shape=tuple(jax.ShapeDtypeStruct(shape, f32) for shape in (out.shape, coef.shape, mask.shape)),
        in_specs=[vmem] * 6,
        out_specs=(hbm, hbm, hbm),
        scratch_shapes=[pltpu.VMEM(mask.shape, f32), dma((6,))],
        compiler_params=pltpu.CompilerParams(vmem_limit_bytes=8 << 20),
    )(out, coef, gather, th_v, tl_v, mask_v)
    return out, coef.T, sea


def solution(mesh):
    in_specs = (
        P("member", "radial", "lateral", None),
        P("member", "radial", "lateral", None),
        P("member"),
        P("radial", "lateral", None),
        P(None, "lateral"),
        P("lateral", None),
    )
    out_specs = (
        P("member", "radial", "lateral", None),
        P("member", ("lateral", "radial")),
        P("lateral", "member"),
    )
    body = functools.partial(shards, mesh.shape["lateral"], mesh.shape["radial"])
    return jax.shard_map(body, mesh=mesh, in_specs=in_specs, out_specs=out_specs, check_vma=False)
```

```python
import functools
import math

import jax
import jax.numpy as jnp
import ml_dtypes
import numpy as np
from jax import lax
from jax.experimental import pallas as pl
from jax.experimental.pallas import tpu as pltpu
from jax.sharding import PartitionSpec as P

MODES = 512
PAD = 8
VMEM = 67043328
MESH = pl.DeviceIdType.MESH
f32, bf16 = jnp.float32, jnp.bfloat16


def halves(table):
    table = table.astype(np.float32)
    high = table.astype(ml_dtypes.bfloat16)
    low = (table - high.astype(np.float32)).astype(ml_dtypes.bfloat16)
    return high, low


def longitude_quarter(count, modes):
    points = np.arange(count // 4)[:, None]
    phase = points * np.arange(modes)[None, :] % count
    angle = 2.0 * math.pi / count * phase
    table = np.concatenate([np.cos(angle), np.sin(angle)], axis=1)
    return halves(table * math.sqrt(2.0 / count))


def colatitude_table(count, modes):
    points = np.arange(count)[:, None]
    phase = np.arange(modes)[None, :] * (2 * points + 1) % (4 * count)
    table = np.cos(math.pi / (2 * count) * phase) * math.sqrt(2.0 / count)
    return halves(table)


def split(x):
    high = x.astype(bf16)
    return high, (x - high.astype(f32)).astype(bf16)


def dot(a, b, dims=(((1,), (0,)), ((), ()))):
    return lax.dot_general(a, b, dims, preferred_element_type=f32)


def choose(index, values):
    bit = 0
    while len(values) > 1:
        odd = (index & (1 << bit)) != 0
        values = [
            jnp.where(odd, values[min(i + 1, len(values) - 1)], values[i])
            for i in range(0, len(values), 2)
        ]
        bit += 1
    return values[0]


def kernel(lat, rad, layers, disp, force, visc, layer, response, mask, trig, cosine,
           out, coef_out, gather, trig_v, mask_v,
           u0, u1, fv, fh, li, he, fsend, frecv, gsend, grecv, resp_v, resp_t, cosine_v, visc_s,
           load_sem, send_sem, x_recv, r_recv, all_recv, far_sem):
    comps, shells, rows, lon = disp.shape
    width = response.shape[1]
    me = lax.axis_index("lateral")
    place = lax.axis_index("radial")
    inner = pl.ds(PAD, rows)
    last = shells - 1
    top = place == rad - 1
    south, north = me < lat - 1, me > 0
    face = jnp.where(top, 0, last)

    def order(i):
        return jnp.where(top, last - i, i)

    def load(source, target, index):
        copy = pltpu.make_async_copy(source, target, load_sem.at[index])
        copy.start()
        return copy

    def arrived(ref, sem):
        pltpu.make_async_copy(ref, ref, sem).wait()

    def peer(d):
        return me ^ d if lat & (lat - 1) == 0 else lax.rem(me + d, lat)

    def around(d, e):
        return {"lateral": peer(d), "radial": lax.rem(place + e, rad)}

    offsets = [(d, e) for d in reversed(range(lat)) for e in range(rad) if d or e]
    barrier = pltpu.get_barrier_semaphore()
    for e in range(1, rad):
        pl.semaphore_signal(barrier, inc=1, device_id=around(0, e), device_id_type=MESH)

    def greet(sem, step):
        @pl.when(me + step < lat)
        def _():
            pl.semaphore_signal(sem, inc=1, device_id={"lateral": me + step}, device_id_type=MESH)

        @pl.when(me >= step)
        def _():
            pl.semaphore_signal(sem, inc=1, device_id={"lateral": me - step}, device_id_type=MESH)

    def greeted(step):
        return jnp.where(me + step < lat, 1, 0) + jnp.where(me >= step, 1, 0)

    greet(barrier, 1)
    steps = [1 << k for k in range((lat - 1).bit_length())]

    c_visc = load(visc, visc_s, 0)
    c_layer = load(layer, li.at[pl.ds(1, shells), inner], 1)
    c_disp = load(disp, u0.at[:, pl.ds(1, shells), inner], 2)
    c_force = load(force, fv, 3)

    void = jnp.where(top, shells + 1, 0)
    tall, wide = rows + 2 * PAD, (1, lon)
    he[void] = jnp.zeros((tall, lon), f32)
    for c in range(comps):
        u0[c, void] = jnp.zeros((tall, lon), f32)
        u1[c, void] = jnp.zeros((tall, lon), f32)

    def unpadded(row):
        for s in range(1, shells + 1):
            he[s, row:row + 1, :] = jnp.zeros(wide, f32)
            for c in range(comps):
                u0[c, s, row:row + 1, :] = jnp.zeros(wide, f32)
                u1[c, s, row:row + 1, :] = jnp.zeros(wide, f32)

    @pl.when(jnp.logical_not(north))
    def _():
        unpadded(PAD - 1)

    @pl.when(jnp.logical_not(south))
    def _():
        unpadded(PAD + rows)

    sides = [
        (0, south, north, jnp.where(south, me + 1, me), pl.ds(rows - 1, 1), pl.ds(rows - 2, 2),
         pl.ds(PAD - 1, 1), pl.ds(PAD - 2, 2), pl.ds(PAD + rows - 1, 1)),
        (1, north, south, jnp.where(north, me - 1, me), pl.ds(0, 1), pl.ds(0, 2),
         pl.ds(PAD + rows, 1), pl.ds(PAD + rows, 2), pl.ds(PAD, 1)),
    ]

    def lateral(side, k, source, target):
        return pltpu.make_async_remote_copy(
            src_ref=source, dst_ref=target, send_sem=send_sem.at[side[0]], recv_sem=x_recv.at[side[0], k],
            device_id={"lateral": side[3]}, device_id_type=MESH)

    def first(side):
        _, _, _, _, one, two, edge, pair, _ = side
        refs = [
            (disp.at[0, last, two], u0.at[0, shells, pair]),
            (layer.at[last, two], li.at[shells, pair]),
            (disp.at[0, last - 1, one], u0.at[0, shells - 1, edge]),
            (layer.at[last - 1, one], li.at[shells - 1, edge]),
            (force.at[0, last, one], fh.at[side[0]]),
        ]
        return [lateral(side, 0, a, b) for a, b in refs]

    rest = pl.ds(1, comps - 1)

    def bulk_rest(side, i):
        s = order(i)
        return [lateral(side, 1 + i, disp.at[rest, s, side[4]], u0.at[rest, s + 1, side[6]])]

    def bulk_all(side, i):
        s = order(i)
        return [lateral(side, 1 + i, layer.at[s, side[4]], li.at[s + 1, side[6]]),
                lateral(side, 1 + i, disp.at[:, s, side[4]], u0.at[:, s + 1, side[6]])]

    def later_rest(side, i):
        s = order(i)
        return [lateral(side, 1 + shells + i, u1.at[rest, s + 1, side[8]], u1.at[rest, s + 1, side[6]])]

    def later_all(side, i):
        s = order(i)
        return [lateral(side, 1 + shells + i, u1.at[:, s + 1, side[8]], u1.at[:, s + 1, side[6]])]

    def for_shell(i, act, some, every):
        alone = jnp.logical_and(top, i < some[1])

        @pl.when(alone)
        def _():
            act(some[0])

        @pl.when(jnp.logical_not(alone))
        def _():
            act(every[0])

    odd = lax.rem(me, 2) == 1

    def nearer_first(go):
        @pl.when(odd)
        def _():
            go(sides[1])

        go(sides[0])

        @pl.when(jnp.logical_not(odd))
        def _():
            go(sides[1])

    def start_to(i, some, every):
        def go(side):
            @pl.when(side[1])
            def _():
                for_shell(i, lambda make: [c.start() for c in make(side, i)], some, every)

        nearer_first(go)

    def got_from(i, k, some, every):
        for side in sides:
            alone = jnp.logical_and(top, i < some[1])
            sem = x_recv.at[side[0], k + i]

            @pl.when(jnp.logical_and(side[2], alone))
            def _():
                arrived(span(some[2]), sem)

            @pl.when(jnp.logical_and(side[2], jnp.logical_not(alone)))
            def _():
                arrived(span(every[1]), sem)

    def span(count):
        parts = min(n for n in range(1, shells + 3) if count % n == 0 and count // n <= 8)
        return u0.at[0, pl.ds(0, parts), pl.ds(0, 8), pl.ds(0, count // parts * (lon // 8))]

    bulk = ((bulk_rest, 2, comps - 1), (bulk_all, comps + 1))
    later = ((later_rest, 1, comps - 1), (later_all, comps))
    rows_first = 7
    rows_top = rows_first + sum(k[0][1] * k[0][2] + (shells - k[0][1]) * k[1][1] for k in (bulk, later))
    rows_other = sum(shells * k[1][1] for k in (bulk, later))

    def across(k, source, target):
        return pltpu.make_async_remote_copy(
            src_ref=source, dst_ref=target, send_sem=send_sem.at[2 + k], recv_sem=r_recv.at[k],
            device_id={"radial": rad - 1 - place}, device_id_type=MESH)

    beyond = jnp.where(top, shells + 1, 0)
    facing = jnp.where(top, 0, shells + 1)
    r_layer = across(0, layer.at[face], li.at[beyond, inner])
    r_disp = across(0, disp.at[:, face], u0.at[:, beyond, inner])
    r_later = across(1, u1.at[:, face + 1, inner], u1.at[:, beyond, inner])

    pl.semaphore_wait(barrier, greeted(1) + rad - 1)

    @pl.when(top)
    def _():
        def go(side):
            @pl.when(side[1])
            def _():
                for copy in first(side):
                    copy.start()

        nearer_first(go)

    r_layer.start()
    r_disp.start()
    greet(far_sem.at[0], steps[0])

    c_visc.wait()
    values = [visc_s[i] * 0.5 for i in range(layers)]

    def lookup_at(s, where):
        he[s, where, :] = choose(li[s, where, :], values)

    def lookup(s):
        for r in range(0, rows, 8):
            lookup_at(s, pl.ds(PAD + r, 8))

    def lookup_step(i, carry):
        lookup(order(i) + 1)
        return carry

    c_layer.wait()
    lax.fori_loop(0, shells, lookup_step, 0)

    start_to(0, *bulk)
    if steps[1:]:
        pl.semaphore_wait(far_sem.at[0], greeted(steps[0]))
        greet(far_sem.at[1], steps[1])

    c_disp.wait()
    c_force.wait()
    start_to(1, *bulk)
    tables = [(trig, trig_v), (response, resp_v), (cosine, cosine_v), (mask, mask_v)]
    c_tables = [load(a, b, 4 + k) for k, (a, b) in enumerate(tables)]

    start_to(2, *bulk)

    chunk = lon // 4

    def beside(load, k):
        first, end = k * chunk, (k + 1) * chunk
        mid = load(slice(first, end))
        before = load(slice((first - 128) % lon, (first - 128) % lon + 128))
        after = load(slice(end % lon, end % lon + 128))
        left = pltpu.roll(jnp.concatenate([before, mid], axis=1), 1, 1)[:, 128:]
        right = pltpu.roll(jnp.concatenate([mid, after], axis=1), chunk + 127, 1)[:, :chunk]
        return mid, left, right

    def sweep(src, s, r, size, some, pushed, store):
        here, next_row, last_row = slice(r, r + size), slice(r + 1, r + size + 1), slice(r - 1, r + size - 1)
        for k in range(4):
            lanes = slice(k * chunk, (k + 1) * chunk)
            h, left, right = beside(lambda cols: he[s + 1, here, cols], k)
            ws = [
                h + he[s + 2, here, lanes],
                h + he[s, here, lanes],
                h + he[s + 1, next_row, lanes],
                h + he[s + 1, last_row, lanes],
                h + left,
                h + right,
            ]
            rate = 0.8 / (1.0 + (((ws[0] + ws[1]) + (ws[2] + ws[3])) + (ws[4] + ws[5])))
            for c in some:
                u, left, right = beside(lambda cols: src[c, s + 1, here, cols], k)
                total = pushed(c, lanes)
                total = total + ws[0] * src[c, s + 2, here, lanes]
                total = total + ws[1] * src[c, s, here, lanes]
                total = total + ws[2] * src[c, s + 1, next_row, lanes]
                total = total + ws[3] * src[c, s + 1, last_row, lanes]
                total = total + ws[4] * left
                total = total + ws[5] * right
                store(c, lanes, 0.2 * u + rate * total)

    def sweep1(s, r, some):
        def store(c, lanes, value):
            u1[c, s + 1, PAD + r:PAD + r + 8, lanes] = value

        sweep(u0, s, PAD + r, 8, some, lambda c, lanes: fv[c, s, r:r + 8, lanes], store)

    def sweep2(s, r, some):
        def store(c, lanes, value):
            out[c, s, r:r + 8, lanes] = value

        sweep(u1, s, PAD + r, 8, some, lambda c, lanes: fv[c, s, r:r + 8, lanes], store)

    edge_rows = sorted({0, rows - 8})
    inner_rows = list(range(8, rows - 8, 8))
    all_comps, rest_comps = list(range(comps)), list(range(1, comps))

    def inner1(i, carry):
        s = order(i)
        for r in inner_rows:
            sweep1(s, r, all_comps)
        return carry

    lax.fori_loop(0, jnp.where(top, 2, 3), inner1, 0)
    for k, step in enumerate(steps):
        if k > 1:
            pl.semaphore_wait(far_sem.at[k - 1], greeted(steps[k - 1]))
            greet(far_sem.at[k], step)

    quarter = lon // 4
    modes = trig.shape[2] // 2
    wave = lax.broadcasted_iota(jnp.int32, (rows, modes), 1) & 3
    zero, one = jnp.zeros((rows, modes), f32), jnp.ones((rows, modes), f32)
    e1 = jnp.where(wave == 0, one, jnp.where(wave == 2, -one, zero))
    s1 = jnp.where(wave == 1, one, jnp.where(wave == 3, -one, zero))
    e2 = jnp.where((wave & 1) == 0, one, -one)
    half = width // rad
    forward = []
    for d, e in [(d, e) for d in reversed(range(lat)) for e in range(rad) if d or e != rad - 1]:
        forward.append((d, e, pltpu.make_async_remote_copy(
            src_ref=fsend.at[peer(d) * rad + e], dst_ref=frecv.at[me],
            send_sem=send_sem.at[4], recv_sem=all_recv.at[0],
            device_id={"lateral": peer(d), "radial": e}, device_id_type=MESH)))

    @pl.when(top)
    def _():
        for side in sides:
            @pl.when(side[2])
            def _():
                arrived(span(rows_first), x_recv.at[side[0], 0])
                lookup_at(shells, side[7])
                lookup_at(shells - 1, side[6])

        def early(i, carry):
            for r in edge_rows:
                sweep1(last - i, r, [0])
            return carry

        lax.fori_loop(0, 2, early, 0)
        for side, row in zip(sides, (PAD - 1, PAD + rows)):
            @pl.when(side[2])
            def _():
                def store(c, lanes, value):
                    u1[c, shells, row:row + 1, lanes] = value

                sweep(u0, last, row, 1, [0], lambda c, lanes: fh[side[0], :, lanes], store)

        for r in range(0, rows, 8):
            sweep2(last, r, [0])

    c_tables[0].wait()

    @pl.when(top)
    def _():
        x = jnp.concatenate([out[0, last, :, quarter * m:quarter * (m + 1)] for m in range(4)], axis=0)
        xh, xl = split(x)
        g = dot(xh, trig_v[0]) + dot(xl, trig_v[0]) + dot(xh, trig_v[1])
        gc = [g[rows * m:rows * (m + 1), :modes] for m in range(4)]
        gs = [g[rows * m:rows * (m + 1), modes:] for m in range(4)]
        fc = gc[0] + e2 * gc[2] + e1 * (gc[1] + gc[3]) - s1 * (gs[1] - gs[3])
        fs = gs[0] + e2 * gs[2] + e1 * (gs[1] + gs[3]) + s1 * (gc[1] - gc[3])
        fourier = jnp.concatenate([fc, fs], axis=1)
        for p in range(lat):
            for e in range(rad):
                fsend[p * rad + e] = fourier[:, p * width + e * half:p * width + (e + 1) * half]

    pl.semaphore_wait(far_sem.at[len(steps) - 1], greeted(steps[-1]))

    @pl.when(top)
    def _():
        for _, _, copy in forward:
            copy.start()
        frecv[me] = fsend[me * rad + rad - 1]

    for i in range(3, shells):
        start_to(i, *bulk)

    def main(i, carry):
        s = order(i)

        @pl.when(i == last)
        def _():
            arrived(u0.at[0, pl.ds(0, comps + 1), inner], r_recv.at[0])
            lookup(facing)

        @pl.when(jnp.logical_or(jnp.logical_and(top, i == 2), i == last))
        def _():
            inner1(i, 0)

        got_from(i, 1, *bulk)
        for side in sides:
            @pl.when(jnp.logical_and(side[2], jnp.logical_not(jnp.logical_and(top, i < 2))))
            def _():
                lookup_at(s + 1, side[6])

        for r in edge_rows:
            sweep1(s, r, all_comps)
        start_to(i, *later)
        return carry

    lax.fori_loop(0, last, main, 0)

    def inner2(i, carry):
        s = order(i)
        alone = jnp.logical_and(top, i == 0)

        @pl.when(alone)
        def _():
            for r in inner_rows:
                sweep2(s, r, rest_comps)

        @pl.when(jnp.logical_not(alone))
        def _():
            for r in inner_rows:
                sweep2(s, r, all_comps)

        return carry

    for copy in c_tables[1:]:
        copy.wait()
    answer = resp_v[:, :half]
    for e in range(1, rad):
        answer = jnp.where(place == e, resp_v[:, e * half:(e + 1) * half], answer)
    resp_t[...] = answer.T

    @pl.when(top)
    def _():
        arrived(frecv.at[pl.ds(0, lat - 1)], all_recv.at[0])

    @pl.when(jnp.logical_not(top))
    def _():
        arrived(frecv, all_recv.at[0])

    spectrum = frecv[...].reshape(lat * rows, half)
    sh, sl = split(spectrum)
    down = (((0,), (0,)), ((), ()))
    both = dot(jnp.concatenate([sh, sl], axis=1), cosine_v[0], down)
    coef = both[:half] + both[half:] + dot(sh, cosine_v[1], down)
    sh, sl = split(resp_t[...] * coef)
    nt = (((1,), (1,)), ((), ()))
    load_rows = dot(cosine_v[0], sh, nt) + dot(cosine_v[0], sl, nt) + dot(cosine_v[1], sh, nt)
    gsend[...] = load_rows.reshape(lat, rows, half)
    back = []
    for d, e in offsets:
        back.append(pltpu.make_async_remote_copy(
            src_ref=gsend.at[peer(d)], dst_ref=grecv.at[me * rad + place],
            send_sem=send_sem.at[5], recv_sem=all_recv.at[1],
            device_id=around(d, e), device_id_type=MESH))
    for copy in back:
        copy.start()
    grecv[me * rad + place] = gsend[me]
    coef_out[...] = coef

    def final(i, carry):
        s = order(i)
        alone = jnp.logical_and(top, i == 0)

        @pl.when(i == last)
        def _():
            r_later.wait_recv()
            inner2(i, 0)

        got_from(i, 1 + shells, *later)

        @pl.when(alone)
        def _():
            for r in edge_rows:
                sweep2(s, r, rest_comps)

        @pl.when(jnp.logical_not(alone))
        def _():
            for r in edge_rows:
                sweep2(s, r, all_comps)

        return carry

    main(last, 0)
    r_later.start()

    lax.fori_loop(0, last, inner2, 0)

    lax.fori_loop(0, shells, final, 0)

    blocks = lat * rad - 1

    @pl.when(top)
    def _():
        arrived(fsend.at[pl.ds(0, blocks)], send_sem.at[4])

    for side in sides:
        for who, count in ((top, rows_top), (jnp.logical_not(top), rows_other)):
            @pl.when(jnp.logical_and(who, side[1]))
            def _():
                arrived(span(count), send_sem.at[side[0]])

    arrived(u0.at[0, pl.ds(0, comps + 1), inner], send_sem.at[2])
    arrived(u0.at[:, 0, inner], send_sem.at[3])
    arrived(grecv.at[pl.ds(0, blocks)], send_sem.at[5])
    arrived(grecv.at[pl.ds(0, blocks)], all_recv.at[1])
    for p in range(lat):
        for e in range(rad):
            gather[:, p * width + e * half:p * width + (e + 1) * half] = grecv[p * rad + e]


def finish(out, coef, gather, trig, mask, out_h, coef_h, sea_h, sea, sem):
    rows, lon = mask.shape
    quarter, modes = lon // 4, trig.shape[2] // 2
    copies = [pltpu.make_async_copy(out, out_h, sem.at[0]), pltpu.make_async_copy(coef, coef_h, sem.at[1])]
    for copy in copies:
        copy.start()
    wave = lax.broadcasted_iota(jnp.int32, (rows, modes), 1) & 3
    zero, one = jnp.zeros((rows, modes), f32), jnp.ones((rows, modes), f32)
    e1 = jnp.where(wave == 0, one, jnp.where(wave == 2, -one, zero))
    s1 = jnp.where(wave == 1, one, jnp.where(wave == 3, -one, zero))
    e2 = jnp.where((wave & 1) == 0, one, -one)
    rc, rs = gather[:, :modes], gather[:, modes:]
    twisted = [
        (rc, rs),
        (e1 * rc + s1 * rs, e1 * rs - s1 * rc),
        (e2 * rc, e2 * rs),
        (e1 * rc - s1 * rs, e1 * rs + s1 * rc),
    ]
    a = jnp.concatenate([jnp.concatenate(pair, axis=1) for pair in twisted], axis=0)
    ah, al = split(a)
    nt = (((1,), (1,)), ((), ()))
    total = dot(ah, trig[0], nt) + dot(al, trig[0], nt) + dot(ah, trig[1], nt)
    for m in range(4):
        cut = slice(quarter * m, quarter * (m + 1))
        sea[:, cut] = mask[:, cut].astype(f32) * total[rows * m:rows * (m + 1)]
        copies.append(pltpu.make_async_copy(sea.at[:, cut], sea_h.at[:, cut], sem.at[2 + m]))
        copies[-1].start()
    for copy in copies:
        copy.wait()


def shards(lat, rad, disp, force, visc, layer, response, mask):
    comps, shells, rows, lon = disp.shape
    width = response.shape[1]
    trig = np.stack(longitude_quarter(lon, MODES))
    cosine = np.stack(colatitude_table(lat * rows, MODES))
    tables = [trig, cosine]
    hbm = pl.BlockSpec(memory_space=pltpu.HBM)
    vmem = pl.BlockSpec(memory_space=pltpu.VMEM)
    tall = rows + 2 * PAD
    field = pltpu.VMEM((comps, shells + 2, tall, lon), f32)
    half = width // rad
    block = pltpu.VMEM((lat, rows, half), f32)
    dma = pltpu.SemaphoreType.DMA
    spare = 4 * (disp.size + MODES * width // rad + 2 * rows * MODES + rows * lon) + 2 * trig.size + 65536
    out, coef, gather, trig_v, mask_v = pl.pallas_call(
        functools.partial(kernel, lat, rad, visc.shape[0]),
        out_shape=(
            pltpu.VMEM(disp.shape, f32),
            pltpu.VMEM((width // rad, MODES), f32),
            pltpu.VMEM((rows, 2 * MODES), f32),
            pltpu.VMEM(trig.shape, bf16),
            pltpu.VMEM(mask.shape, jnp.int32),
        ),
        in_specs=[hbm] * 8,
        out_specs=(vmem,) * 5,
        scratch_shapes=[
            field, field,
            pltpu.VMEM((comps, shells, rows, lon), f32),
            pltpu.VMEM((2, 1, lon), f32),
            pltpu.VMEM((shells + 2, tall, lon), jnp.int32),
            pltpu.VMEM((shells + 2, tall, lon), f32),
            pltpu.VMEM((lat * rad, rows, half), f32), block, block, pltpu.VMEM((lat * rad, rows, half), f32),
            pltpu.VMEM(response.shape, f32), pltpu.VMEM((half, MODES), f32),
            pltpu.VMEM(cosine.shape, bf16),
            pltpu.SMEM(visc.shape, f32),
            dma((8,)), dma((6,)), dma((2, 1 + 2 * shells)), dma((2,)), dma((2,)),
            pltpu.SemaphoreType.REGULAR((max(1, (lat - 1).bit_length()),)),
        ],
        compiler_params=pltpu.CompilerParams(
            collective_id=0, has_side_effects=True, vmem_limit_bytes=VMEM - spare),
    )(disp, force, visc, layer, response, mask, *[jnp.asarray(t) for t in tables])
    out, coef, sea = pl.pallas_call(
        finish,
        out_shape=tuple(jax.ShapeDtypeStruct(shape, f32) for shape in (out.shape, coef.shape, mask.shape)),
        in_specs=[vmem] * 5,
        out_specs=(hbm, hbm, hbm),
        scratch_shapes=[pltpu.VMEM(mask.shape, f32), dma((6,))],
        compiler_params=pltpu.CompilerParams(vmem_limit_bytes=8 << 20),
    )(out, coef, gather, trig_v, mask_v)
    return out, coef.T, sea


def solution(mesh):
    in_specs = (
        P("member", "radial", "lateral", None),
        P("member", "radial", "lateral", None),
        P("member"),
        P("radial", "lateral", None),
        P(None, "lateral"),
        P("lateral", None),
    )
    out_specs = (
        P("member", "radial", "lateral", None),
        P("member", ("lateral", "radial")),
        P("lateral", "member"),
    )
    body = functools.partial(shards, mesh.shape["lateral"], mesh.shape["radial"])
    return jax.shard_map(body, mesh=mesh, in_specs=in_specs, out_specs=out_specs, check_vma=False)
```

```python
import functools
import math

import jax
import jax.numpy as jnp
import ml_dtypes
import numpy as np
from jax import lax
from jax.experimental import pallas as pl
from jax.experimental.pallas import tpu as pltpu
from jax.sharding import PartitionSpec as P

MODES = 512
PAD = 8
VMEM = 67043328
MESH = pl.DeviceIdType.MESH
f32, bf16 = jnp.float32, jnp.bfloat16


def halves(table):
    table = table.astype(np.float32)
    high = table.astype(ml_dtypes.bfloat16)
    low = (table - high.astype(np.float32)).astype(ml_dtypes.bfloat16)
    return high, low


def longitude_quarter(count, modes):
    points = np.arange(count // 4)[:, None]
    phase = points * np.arange(modes)[None, :] % count
    angle = 2.0 * math.pi / count * phase
    table = np.concatenate([np.cos(angle), np.sin(angle)], axis=1)
    return halves(table * math.sqrt(2.0 / count))


def colatitude_table(count, modes):
    points = np.arange(count)[:, None]
    phase = np.arange(modes)[None, :] * (2 * points + 1) % (4 * count)
    table = np.cos(math.pi / (2 * count) * phase) * math.sqrt(2.0 / count)
    return halves(table)


def split(x):
    high = x.astype(bf16)
    return high, (x - high.astype(f32)).astype(bf16)


def dot(a, b, dims=(((1,), (0,)), ((), ()))):
    return lax.dot_general(a, b, dims, preferred_element_type=f32)


def swap(a, b):
    half = a.shape[-1] // 2
    low = lax.broadcasted_iota(jnp.int32, a.shape, a.ndim - 1) < half
    return jnp.where(low, a, pltpu.roll(b, half, a.ndim - 1)), jnp.where(low, pltpu.roll(a, half, a.ndim - 1), b)


def choose(index, values):
    bit = 0
    while len(values) > 1:
        odd = (index & (1 << bit)) != 0
        values = [
            jnp.where(odd, values[min(i + 1, len(values) - 1)], values[i])
            for i in range(0, len(values), 2)
        ]
        bit += 1
    return values[0]


def kernel(lat, rad, layers, disp, force, visc, layer, response, mask, trig, cosine,
           out, coef_out, gather, trig_v, mask_v,
           u0, u1, fv, fh, li, he, fsend, frecv, gsend, grecv, resp_v, resp_t, cosine_v, visc_s,
           load_sem, send_sem, x_recv, r_recv, all_recv, far_sem):
    comps, shells, rows, lon = disp.shape
    width = response.shape[1]
    me = lax.axis_index("lateral")
    place = lax.axis_index("radial")
    inner = pl.ds(PAD, rows)
    last = shells - 1
    top = place == rad - 1
    south, north = me < lat - 1, me > 0
    face = jnp.where(top, 0, last)

    def order(i):
        return jnp.where(top, last - i, i)

    def load(source, target, index):
        copy = pltpu.make_async_copy(source, target, load_sem.at[index])
        copy.start()
        return copy

    def arrived(ref, sem):
        pltpu.make_async_copy(ref, ref, sem).wait()

    def peer(d):
        return me ^ d if lat & (lat - 1) == 0 else lax.rem(me + d, lat)

    def around(d, e):
        return {"lateral": peer(d), "radial": lax.rem(place + e, rad)}

    offsets = [(d, e) for d in reversed(range(lat)) for e in range(rad) if d or e]
    barrier = pltpu.get_barrier_semaphore()
    for e in range(1, rad):
        pl.semaphore_signal(barrier, inc=1, device_id=around(0, e), device_id_type=MESH)

    def greet(sem, step):
        @pl.when(me + step < lat)
        def _():
            pl.semaphore_signal(sem, inc=1, device_id={"lateral": me + step}, device_id_type=MESH)

        @pl.when(me >= step)
        def _():
            pl.semaphore_signal(sem, inc=1, device_id={"lateral": me - step}, device_id_type=MESH)

    def greeted(step):
        return jnp.where(me + step < lat, 1, 0) + jnp.where(me >= step, 1, 0)

    greet(barrier, 1)
    steps = [1 << k for k in range((lat - 1).bit_length())]

    c_visc = load(visc, visc_s, 0)
    c_layer = load(layer, li.at[pl.ds(1, shells), inner], 1)
    c_disp = load(disp, u0.at[:, pl.ds(1, shells), inner], 2)
    c_force = load(force, fv, 3)

    void = jnp.where(top, shells + 1, 0)
    tall, wide = rows + 2 * PAD, (1, lon)
    he[void] = jnp.zeros((tall, lon), f32)
    for c in range(comps):
        u0[c, void] = jnp.zeros((tall, lon), f32)
        u1[c, void] = jnp.zeros((tall, lon), f32)

    def unpadded(row):
        for s in range(1, shells + 1):
            he[s, row:row + 1, :] = jnp.zeros(wide, f32)
            for c in range(comps):
                u0[c, s, row:row + 1, :] = jnp.zeros(wide, f32)
                u1[c, s, row:row + 1, :] = jnp.zeros(wide, f32)

    @pl.when(jnp.logical_not(north))
    def _():
        unpadded(PAD - 1)

    @pl.when(jnp.logical_not(south))
    def _():
        unpadded(PAD + rows)

    sides = [
        (0, south, north, jnp.where(south, me + 1, me), pl.ds(rows - 1, 1), pl.ds(rows - 2, 2),
         pl.ds(PAD - 1, 1), pl.ds(PAD - 2, 2), pl.ds(PAD + rows - 1, 1)),
        (1, north, south, jnp.where(north, me - 1, me), pl.ds(0, 1), pl.ds(0, 2),
         pl.ds(PAD + rows, 1), pl.ds(PAD + rows, 2), pl.ds(PAD, 1)),
    ]

    def lateral(side, k, source, target):
        return pltpu.make_async_remote_copy(
            src_ref=source, dst_ref=target, send_sem=send_sem.at[side[0]], recv_sem=x_recv.at[side[0], k],
            device_id={"lateral": side[3]}, device_id_type=MESH)

    def first(side):
        _, _, _, _, one, two, edge, pair, _ = side
        refs = [
            (disp.at[0, last, two], u0.at[0, shells, pair]),
            (layer.at[last, two], li.at[shells, pair]),
            (disp.at[0, last - 1, one], u0.at[0, shells - 1, edge]),
            (layer.at[last - 1, one], li.at[shells - 1, edge]),
            (force.at[0, last, one], fh.at[side[0]]),
        ]
        return [lateral(side, 0, a, b) for a, b in refs]

    rest = pl.ds(1, comps - 1)

    def bulk_rest(side, i):
        s = order(i)
        return [lateral(side, 1 + i, disp.at[rest, s, side[4]], u0.at[rest, s + 1, side[6]])]

    def bulk_all(side, i):
        s = order(i)
        return [lateral(side, 1 + i, layer.at[s, side[4]], li.at[s + 1, side[6]]),
                lateral(side, 1 + i, disp.at[:, s, side[4]], u0.at[:, s + 1, side[6]])]

    def later_rest(side, i):
        s = order(i)
        return [lateral(side, 1 + shells + i, u1.at[rest, s + 1, side[8]], u1.at[rest, s + 1, side[6]])]

    def later_all(side, i):
        s = order(i)
        return [lateral(side, 1 + shells + i, u1.at[:, s + 1, side[8]], u1.at[:, s + 1, side[6]])]

    def for_shell(i, act, some, every):
        alone = jnp.logical_and(top, i < some[1])

        @pl.when(alone)
        def _():
            act(some[0])

        @pl.when(jnp.logical_not(alone))
        def _():
            act(every[0])

    odd = lax.rem(me, 2) == 1

    def nearer_first(go):
        @pl.when(odd)
        def _():
            go(sides[1])

        go(sides[0])

        @pl.when(jnp.logical_not(odd))
        def _():
            go(sides[1])

    def start_to(i, some, every):
        def go(side):
            @pl.when(side[1])
            def _():
                for_shell(i, lambda make: [c.start() for c in make(side, i)], some, every)

        nearer_first(go)

    def got_from(i, k, some, every):
        for side in sides:
            alone = jnp.logical_and(top, i < some[1])
            sem = x_recv.at[side[0], k + i]

            @pl.when(jnp.logical_and(side[2], alone))
            def _():
                arrived(span(some[2]), sem)

            @pl.when(jnp.logical_and(side[2], jnp.logical_not(alone)))
            def _():
                arrived(span(every[1]), sem)

    def span(count):
        parts = min(n for n in range(1, shells + 3) if count % n == 0 and count // n <= 8)
        return u0.at[0, pl.ds(0, parts), pl.ds(0, 8), pl.ds(0, count // parts * (lon // 8))]

    bulk = ((bulk_rest, 2, comps - 1), (bulk_all, comps + 1))
    later = ((later_rest, 1, comps - 1), (later_all, comps))
    rows_first = 7
    rows_top = rows_first + sum(k[0][1] * k[0][2] + (shells - k[0][1]) * k[1][1] for k in (bulk, later))
    rows_other = sum(shells * k[1][1] for k in (bulk, later))

    def across(k, source, target):
        return pltpu.make_async_remote_copy(
            src_ref=source, dst_ref=target, send_sem=send_sem.at[2 + k], recv_sem=r_recv.at[k],
            device_id={"radial": rad - 1 - place}, device_id_type=MESH)

    beyond = jnp.where(top, shells + 1, 0)
    facing = jnp.where(top, 0, shells + 1)
    r_layer = across(0, layer.at[face], li.at[beyond, inner])
    r_disp = across(0, disp.at[:, face], u0.at[:, beyond, inner])
    r_later = across(1, u1.at[:, face + 1, inner], u1.at[:, beyond, inner])

    pl.semaphore_wait(barrier, greeted(1) + rad - 1)

    @pl.when(top)
    def _():
        def go(side):
            @pl.when(side[1])
            def _():
                for copy in first(side):
                    copy.start()

        nearer_first(go)

    r_layer.start()
    r_disp.start()
    greet(far_sem.at[0], steps[0])

    c_visc.wait()
    values = [visc_s[i] * 0.5 for i in range(layers)]

    def lookup_at(s, where):
        he[s, where, :] = choose(li[s, where, :], values)

    def lookup(s):
        for r in range(0, rows, 8):
            lookup_at(s, pl.ds(PAD + r, 8))

    def lookup_step(i, carry):
        lookup(order(i) + 1)
        return carry

    c_layer.wait()
    lax.fori_loop(0, shells, lookup_step, 0)

    start_to(0, *bulk)
    if steps[1:]:
        pl.semaphore_wait(far_sem.at[0], greeted(steps[0]))
        greet(far_sem.at[1], steps[1])

    c_disp.wait()
    c_force.wait()
    start_to(1, *bulk)
    tables = [(trig, trig_v), (response, resp_v), (cosine, cosine_v), (mask, mask_v)]
    c_tables = [load(a, b, 4 + k) for k, (a, b) in enumerate(tables)]

    start_to(2, *bulk)

    chunk = lon // 4

    def beside(load, k):
        first, end = k * chunk, (k + 1) * chunk
        mid = load(slice(first, end))
        before = load(slice((first - 128) % lon, (first - 128) % lon + 128))
        after = load(slice(end % lon, end % lon + 128))
        left = pltpu.roll(jnp.concatenate([before, mid], axis=1), 1, 1)[:, 128:]
        right = pltpu.roll(jnp.concatenate([mid, after], axis=1), chunk + 127, 1)[:, :chunk]
        return mid, left, right

    def sweep(src, s, r, size, some, pushed, store):
        here, next_row, last_row = slice(r, r + size), slice(r + 1, r + size + 1), slice(r - 1, r + size - 1)
        for k in range(4):
            lanes = slice(k * chunk, (k + 1) * chunk)
            h, left, right = beside(lambda cols: he[s + 1, here, cols], k)
            ws = [
                h + he[s + 2, here, lanes],
                h + he[s, here, lanes],
                h + he[s + 1, next_row, lanes],
                h + he[s + 1, last_row, lanes],
                h + left,
                h + right,
            ]
            rate = 0.8 / (1.0 + (((ws[0] + ws[1]) + (ws[2] + ws[3])) + (ws[4] + ws[5])))
            for c in some:
                u, left, right = beside(lambda cols: src[c, s + 1, here, cols], k)
                total = pushed(c, lanes)
                total = total + ws[0] * src[c, s + 2, here, lanes]
                total = total + ws[1] * src[c, s, here, lanes]
                total = total + ws[2] * src[c, s + 1, next_row, lanes]
                total = total + ws[3] * src[c, s + 1, last_row, lanes]
                total = total + ws[4] * left
                total = total + ws[5] * right
                store(c, lanes, 0.2 * u + rate * total)

    def sweep1(s, r, some):
        def store(c, lanes, value):
            u1[c, s + 1, PAD + r:PAD + r + 8, lanes] = value

        sweep(u0, s, PAD + r, 8, some, lambda c, lanes: fv[c, s, r:r + 8, lanes], store)

    def sweep2(s, r, some):
        def store(c, lanes, value):
            out[c, s, r:r + 8, lanes] = value

        sweep(u1, s, PAD + r, 8, some, lambda c, lanes: fv[c, s, r:r + 8, lanes], store)

    edge_rows = sorted({0, rows - 8})
    inner_rows = list(range(8, rows - 8, 8))
    all_comps, rest_comps = list(range(comps)), list(range(1, comps))

    def inner1(i, carry):
        s = order(i)
        for r in inner_rows:
            sweep1(s, r, all_comps)
        return carry

    ready = jnp.where(top, 2, last)
    lax.fori_loop(0, ready, inner1, 0)
    for k, step in enumerate(steps):
        if k > 1:
            pl.semaphore_wait(far_sem.at[k - 1], greeted(steps[k - 1]))
            greet(far_sem.at[k], step)

    quarter = lon // 4
    modes = trig.shape[2] // 2
    wave = lax.broadcasted_iota(jnp.int32, (rows, modes), 1) & 3
    zero, one = jnp.zeros((rows, modes), f32), jnp.ones((rows, modes), f32)
    e1 = jnp.where(wave == 0, one, jnp.where(wave == 2, -one, zero))
    s1 = jnp.where(wave == 1, one, jnp.where(wave == 3, -one, zero))
    e2 = jnp.where((wave & 1) == 0, one, -one)
    half = width // rad
    forward = []
    for d, e in [(d, e) for d in reversed(range(lat)) for e in range(rad) if d or e != rad - 1]:
        forward.append((d, e, pltpu.make_async_remote_copy(
            src_ref=fsend.at[peer(d) * rad + e], dst_ref=frecv.at[me],
            send_sem=send_sem.at[4], recv_sem=all_recv.at[0],
            device_id={"lateral": peer(d), "radial": e}, device_id_type=MESH)))

    @pl.when(top)
    def _():
        for side in sides:
            @pl.when(side[2])
            def _():
                arrived(span(rows_first), x_recv.at[side[0], 0])
                lookup_at(shells, side[7])
                lookup_at(shells - 1, side[6])

        def early(i, carry):
            for r in edge_rows:
                sweep1(last - i, r, [0])
            return carry

        lax.fori_loop(0, 2, early, 0)
        for side, row in zip(sides, (PAD - 1, PAD + rows)):
            @pl.when(side[2])
            def _():
                def store(c, lanes, value):
                    u1[c, shells, row:row + 1, lanes] = value

                sweep(u0, last, row, 1, [0], lambda c, lanes: fh[side[0], :, lanes], store)

        for r in range(0, rows, 8):
            sweep2(last, r, [0])

    c_tables[0].wait()

    @pl.when(top)
    def _():
        x = jnp.concatenate([out[0, last, :, quarter * m:quarter * (m + 1)] for m in range(4)], axis=0)
        xh, xl = split(x)
        g = dot(xh, trig_v[0]) + dot(xl, trig_v[0]) + dot(xh, trig_v[1])
        gc = [g[rows * m:rows * (m + 1), :modes] for m in range(4)]
        gs = [g[rows * m:rows * (m + 1), modes:] for m in range(4)]
        fc = gc[0] + e2 * gc[2] + e1 * (gc[1] + gc[3]) - s1 * (gs[1] - gs[3])
        fs = gs[0] + e2 * gs[2] + e1 * (gs[1] + gs[3]) + s1 * (gc[1] - gc[3])
        fourier = jnp.concatenate([fc, fs], axis=1)
        for p in range(lat):
            cols = slice(p * width, (p + 1) * width)
            fsend[p * rad], fsend[p * rad + 1] = swap(fourier[:rows // 2, cols], fourier[rows // 2:, cols])

    pl.semaphore_wait(far_sem.at[len(steps) - 1], greeted(steps[-1]))

    @pl.when(top)
    def _():
        for _, _, copy in forward:
            copy.start()
        frecv[me] = fsend[me * rad + rad - 1]

    for i in range(3, shells):
        start_to(i, *bulk)

    def main(i, carry):
        s = order(i)

        got_from(i, 1, *bulk)
        for side in sides:
            @pl.when(jnp.logical_and(side[2], jnp.logical_not(jnp.logical_and(top, i < 2))))
            def _():
                lookup_at(s + 1, side[6])

        for r in edge_rows:
            sweep1(s, r, all_comps)
        start_to(i, *later)
        return carry

    def inner2(i, carry):
        s = order(i)
        alone = jnp.logical_and(top, i == 0)

        @pl.when(alone)
        def _():
            for r in inner_rows:
                sweep2(s, r, rest_comps)

        @pl.when(jnp.logical_not(alone))
        def _():
            for r in inner_rows:
                sweep2(s, r, all_comps)

        return carry

    lax.fori_loop(0, 2, main, 0)
    arrived(u0.at[0, pl.ds(0, comps + 1), inner], r_recv.at[0])
    lookup(facing)
    lax.fori_loop(ready, shells, inner1, 0)
    inner2(0, 0)

    for copy in c_tables[1:]:
        copy.wait()
    answer = resp_v[:, :half]
    for e in range(1, rad):
        answer = jnp.where(place == e, resp_v[:, e * half:(e + 1) * half], answer)
    resp_t[...] = answer.T

    @pl.when(top)
    def _():
        arrived(frecv.at[pl.ds(0, lat - 1)], all_recv.at[0])

    @pl.when(jnp.logical_not(top))
    def _():
        arrived(frecv, all_recv.at[0])

    packed = frecv[...].reshape(lat * rows // 2, width)
    spectrum = jnp.concatenate([packed, pltpu.roll(packed, half, 1)], axis=0)
    low = lax.broadcasted_iota(jnp.int32, spectrum.shape, 1) < half
    sh = spectrum.astype(bf16).astype(f32)
    both = jnp.where(low, sh, pltpu.roll(spectrum - sh, half, 1)).astype(bf16)
    down = (((0,), (0,)), ((), ()))
    coef = dot(both, cosine_v[0], down)
    coef = coef[:half] + coef[half:] + dot(both[:, :half], cosine_v[1], down)
    sh, sl = split(resp_t[...] * coef)
    nt = (((1,), (1,)), ((), ()))
    load_rows = dot(cosine_v[0], jnp.concatenate([sh, sl], axis=0), nt)
    load_rows = load_rows + pltpu.roll(load_rows, half, 1) + dot(cosine_v[1], jnp.concatenate([sh, sh], axis=0), nt)
    upper, lower = load_rows[:lat * rows // 2], load_rows[lat * rows // 2:]
    gsend[...] = jnp.where(low[:lat * rows // 2], upper, lower).reshape(lat, rows // 2, width)
    back = []
    for d, e in offsets:
        back.append(pltpu.make_async_remote_copy(
            src_ref=gsend.at[peer(d)], dst_ref=grecv.at[me * rad + place],
            send_sem=send_sem.at[5], recv_sem=all_recv.at[1],
            device_id=around(d, e), device_id_type=MESH))
    for copy in back:
        copy.start()
    grecv[me * rad + place] = gsend[me]
    coef_out[...] = coef

    def final(i, carry):
        s = order(i)
        alone = jnp.logical_and(top, i == 0)

        @pl.when(i == last)
        def _():
            r_later.wait_recv()
            inner2(i, 0)

        got_from(i, 1 + shells, *later)

        @pl.when(alone)
        def _():
            for r in edge_rows:
                sweep2(s, r, rest_comps)

        @pl.when(jnp.logical_not(alone))
        def _():
            for r in edge_rows:
                sweep2(s, r, all_comps)

        return carry

    lax.fori_loop(2, shells, main, 0)
    r_later.start()

    lax.fori_loop(1, last, inner2, 0)


    lax.fori_loop(0, shells, final, 0)

    blocks = lat * rad - 1

    @pl.when(top)
    def _():
        arrived(fsend.at[pl.ds(0, blocks)], send_sem.at[4])

    for side in sides:
        for who, count in ((top, rows_top), (jnp.logical_not(top), rows_other)):
            @pl.when(jnp.logical_and(who, side[1]))
            def _():
                arrived(span(count), send_sem.at[side[0]])

    arrived(u0.at[0, pl.ds(0, comps + 1), inner], send_sem.at[2])
    arrived(u0.at[:, 0, inner], send_sem.at[3])
    arrived(grecv.at[pl.ds(0, blocks)], send_sem.at[5])
    arrived(grecv.at[pl.ds(0, blocks)], all_recv.at[1])
    for p in range(lat):
        cols = slice(p * width, (p + 1) * width)
        gather[:rows // 2, cols], gather[rows // 2:, cols] = swap(grecv[p * rad], grecv[p * rad + 1])


def finish(out, coef, gather, trig, mask, out_h, coef_h, sea_h, sea, sem):
    rows, lon = mask.shape
    quarter, modes = lon // 4, trig.shape[2] // 2
    copies = [pltpu.make_async_copy(out, out_h, sem.at[0]), pltpu.make_async_copy(coef, coef_h, sem.at[1])]
    for copy in copies:
        copy.start()
    wave = lax.broadcasted_iota(jnp.int32, (rows, modes), 1) & 3
    zero, one = jnp.zeros((rows, modes), f32), jnp.ones((rows, modes), f32)
    e1 = jnp.where(wave == 0, one, jnp.where(wave == 2, -one, zero))
    s1 = jnp.where(wave == 1, one, jnp.where(wave == 3, -one, zero))
    e2 = jnp.where((wave & 1) == 0, one, -one)
    rc, rs = gather[:, :modes], gather[:, modes:]
    twisted = [
        (rc, rs),
        (e1 * rc + s1 * rs, e1 * rs - s1 * rc),
        (e2 * rc, e2 * rs),
        (e1 * rc - s1 * rs, e1 * rs + s1 * rc),
    ]
    a = jnp.concatenate([jnp.concatenate(pair, axis=1) for pair in twisted], axis=0)
    ah, al = split(a)
    nt = (((1,), (1,)), ((), ()))
    total = dot(ah, trig[0], nt) + dot(al, trig[0], nt) + dot(ah, trig[1], nt)
    for m in range(4):
        cut = slice(quarter * m, quarter * (m + 1))
        sea[:, cut] = mask[:, cut].astype(f32) * total[rows * m:rows * (m + 1)]
        copies.append(pltpu.make_async_copy(sea.at[:, cut], sea_h.at[:, cut], sem.at[2 + m]))
        copies[-1].start()
    for copy in copies:
        copy.wait()


def shards(lat, rad, disp, force, visc, layer, response, mask):
    comps, shells, rows, lon = disp.shape
    width = response.shape[1]
    trig = np.stack(longitude_quarter(lon, MODES))
    cosine = np.stack(colatitude_table(lat * rows, MODES)).reshape(2, lat, 2, rows // 2, MODES)
    cosine = cosine.transpose(0, 2, 1, 3, 4).reshape(2, lat * rows, MODES)
    tables = [trig, cosine]
    hbm = pl.BlockSpec(memory_space=pltpu.HBM)
    vmem = pl.BlockSpec(memory_space=pltpu.VMEM)
    tall = rows + 2 * PAD
    field = pltpu.VMEM((comps, shells + 2, tall, lon), f32)
    half = width // rad
    block = pltpu.VMEM((lat, rows // 2, width), f32)
    blocks = pltpu.VMEM((lat * rad, rows // 2, width), f32)
    dma = pltpu.SemaphoreType.DMA
    spare = 4 * (disp.size + MODES * width // rad + 2 * rows * MODES + rows * lon) + 2 * trig.size + 65536
    out, coef, gather, trig_v, mask_v = pl.pallas_call(
        functools.partial(kernel, lat, rad, visc.shape[0]),
        out_shape=(
            pltpu.VMEM(disp.shape, f32),
            pltpu.VMEM((width // rad, MODES), f32),
            pltpu.VMEM((rows, 2 * MODES), f32),
            pltpu.VMEM(trig.shape, bf16),
            pltpu.VMEM(mask.shape, jnp.int32),
        ),
        in_specs=[hbm] * 8,
        out_specs=(vmem,) * 5,
        scratch_shapes=[
            field, field,
            pltpu.VMEM((comps, shells, rows, lon), f32),
            pltpu.VMEM((2, 1, lon), f32),
            pltpu.VMEM((shells + 2, tall, lon), jnp.int32),
            pltpu.VMEM((shells + 2, tall, lon), f32),
            blocks, block, block, blocks,
            pltpu.VMEM(response.shape, f32), pltpu.VMEM((half, MODES), f32),
            pltpu.VMEM(cosine.shape, bf16),
            pltpu.SMEM(visc.shape, f32),
            dma((8,)), dma((6,)), dma((2, 1 + 2 * shells)), dma((2,)), dma((2,)),
            pltpu.SemaphoreType.REGULAR((max(1, (lat - 1).bit_length()),)),
        ],
        compiler_params=pltpu.CompilerParams(
            collective_id=0, has_side_effects=True, vmem_limit_bytes=VMEM - spare),
    )(disp, force, visc, layer, response, mask, *[jnp.asarray(t) for t in tables])
    out, coef, sea = pl.pallas_call(
        finish,
        out_shape=tuple(jax.ShapeDtypeStruct(shape, f32) for shape in (out.shape, coef.shape, mask.shape)),
        in_specs=[vmem] * 5,
        out_specs=(hbm, hbm, hbm),
        scratch_shapes=[pltpu.VMEM(mask.shape, f32), dma((6,))],
        compiler_params=pltpu.CompilerParams(vmem_limit_bytes=8 << 20),
    )(out, coef, gather, trig_v, mask_v)
    return out, coef.T, sea


def solution(mesh):
    in_specs = (
        P("member", "radial", "lateral", None),
        P("member", "radial", "lateral", None),
        P("member"),
        P("radial", "lateral", None),
        P(None, "lateral"),
        P("lateral", None),
    )
    out_specs = (
        P("member", "radial", "lateral", None),
        P("member", ("lateral", "radial")),
        P("lateral", "member"),
    )
    body = functools.partial(shards, mesh.shape["lateral"], mesh.shape["radial"])
    return jax.shard_map(body, mesh=mesh, in_specs=in_specs, out_specs=out_specs, check_vma=False)
```

```python
import functools
import math

import jax
import jax.numpy as jnp
import ml_dtypes
import numpy as np
from jax import lax
from jax.experimental import pallas as pl
from jax.experimental.pallas import tpu as pltpu
from jax.sharding import PartitionSpec as P

MODES = 512
PAD = 8
VMEM = 67043328
MESH = pl.DeviceIdType.MESH
f32, bf16 = jnp.float32, jnp.bfloat16


def halves(table):
    table = table.astype(np.float32)
    high = table.astype(ml_dtypes.bfloat16)
    low = (table - high.astype(np.float32)).astype(ml_dtypes.bfloat16)
    return high, low


def longitude_quarter(count, modes):
    points = np.arange(count // 4)[:, None]
    phase = points * np.arange(modes)[None, :] % count
    angle = 2.0 * math.pi / count * phase
    table = np.concatenate([np.cos(angle), np.sin(angle)], axis=1)
    return halves(table * math.sqrt(2.0 / count))


def colatitude_table(count, modes):
    points = np.arange(count)[:, None]
    phase = np.arange(modes)[None, :] * (2 * points + 1) % (4 * count)
    table = np.cos(math.pi / (2 * count) * phase) * math.sqrt(2.0 / count)
    return halves(table)


def split(x):
    high = x.astype(bf16)
    return high, (x - high.astype(f32)).astype(bf16)


def dot(a, b, dims=(((1,), (0,)), ((), ()))):
    return lax.dot_general(a, b, dims, preferred_element_type=f32)


def swap(a, b):
    half = a.shape[-1] // 2
    low = lax.broadcasted_iota(jnp.int32, a.shape, a.ndim - 1) < half
    return jnp.where(low, a, pltpu.roll(b, half, a.ndim - 1)), jnp.where(low, pltpu.roll(a, half, a.ndim - 1), b)


def choose(index, values):
    bit = 0
    while len(values) > 1:
        odd = (index & (1 << bit)) != 0
        values = [
            jnp.where(odd, values[min(i + 1, len(values) - 1)], values[i])
            for i in range(0, len(values), 2)
        ]
        bit += 1
    return values[0]


def kernel(lat, rad, layers, disp, force, visc, layer, response, mask, trig, cosine,
           out, coef_out, gather, trig_v, mask_v,
           u0, u1, fv, fh, li, he, fsend, frecv, gsend, grecv, resp_v, resp_t, cosine_v, visc_s,
           load_sem, send_sem, x_recv, r_recv, all_recv, far_sem):
    comps, shells, rows, lon = disp.shape
    width = response.shape[1]
    me = lax.axis_index("lateral")
    place = lax.axis_index("radial")
    inner = pl.ds(PAD, rows)
    last = shells - 1
    top = place == rad - 1
    south, north = me < lat - 1, me > 0
    face = jnp.where(top, 0, last)

    def order(i):
        return jnp.where(top, last - i, i)

    def load(source, target, index):
        copy = pltpu.make_async_copy(source, target, load_sem.at[index])
        copy.start()
        return copy

    def arrived(ref, sem):
        pltpu.make_async_copy(ref, ref, sem).wait()

    def peer(d):
        return me ^ d if lat & (lat - 1) == 0 else lax.rem(me + d, lat)

    def around(d, e):
        return {"lateral": peer(d), "radial": lax.rem(place + e, rad)}

    offsets = [(d, e) for d in reversed(range(lat)) for e in range(rad) if d or e]
    quarters = max(1, lat // 4)
    middle = jnp.logical_and(me >= quarters, me < lat - quarters)

    def far_first(copies):
        for here, rank in ((middle, [2, 3, 1, 0]), (jnp.logical_not(middle), [3, 2, 1, 0])):
            @pl.when(here)
            def _():
                for _, copy in sorted(copies, key=lambda pair: rank.index(min(3, pair[0] // quarters))):
                    copy.start()

    barrier = pltpu.get_barrier_semaphore()
    for e in range(1, rad):
        pl.semaphore_signal(barrier, inc=1, device_id=around(0, e), device_id_type=MESH)

    def greet(sem, step):
        @pl.when(me + step < lat)
        def _():
            pl.semaphore_signal(sem, inc=1, device_id={"lateral": me + step}, device_id_type=MESH)

        @pl.when(me >= step)
        def _():
            pl.semaphore_signal(sem, inc=1, device_id={"lateral": me - step}, device_id_type=MESH)

    def greeted(step):
        return jnp.where(me + step < lat, 1, 0) + jnp.where(me >= step, 1, 0)

    greet(barrier, 1)
    steps = [1 << k for k in range((lat - 1).bit_length())]

    c_visc = load(visc, visc_s, 0)
    c_layer = load(layer, li.at[pl.ds(1, shells), inner], 1)
    rest = pl.ds(1, comps - 1)
    c_first = [load(disp.at[0], u0.at[0, pl.ds(1, shells), inner], 2), load(force.at[0], fv.at[0], 3)]

    void = jnp.where(top, shells + 1, 0)
    tall, wide = rows + 2 * PAD, (1, lon)
    he[void] = jnp.zeros((tall, lon), f32)
    for c in range(comps):
        u0[c, void] = jnp.zeros((tall, lon), f32)
        u1[c, void] = jnp.zeros((tall, lon), f32)

    def unpadded(row):
        for s in range(1, shells + 1):
            he[s, row:row + 1, :] = jnp.zeros(wide, f32)
            for c in range(comps):
                u0[c, s, row:row + 1, :] = jnp.zeros(wide, f32)
                u1[c, s, row:row + 1, :] = jnp.zeros(wide, f32)

    @pl.when(jnp.logical_not(north))
    def _():
        unpadded(PAD - 1)

    @pl.when(jnp.logical_not(south))
    def _():
        unpadded(PAD + rows)

    sides = [
        (0, south, north, jnp.where(south, me + 1, me), pl.ds(rows - 1, 1), pl.ds(rows - 2, 2),
         pl.ds(PAD - 1, 1), pl.ds(PAD - 2, 2), pl.ds(PAD + rows - 1, 1)),
        (1, north, south, jnp.where(north, me - 1, me), pl.ds(0, 1), pl.ds(0, 2),
         pl.ds(PAD + rows, 1), pl.ds(PAD + rows, 2), pl.ds(PAD, 1)),
    ]

    def lateral(side, k, source, target):
        return pltpu.make_async_remote_copy(
            src_ref=source, dst_ref=target, send_sem=send_sem.at[side[0]], recv_sem=x_recv.at[side[0], k],
            device_id={"lateral": side[3]}, device_id_type=MESH)

    def first(side):
        _, _, _, _, one, two, edge, pair, _ = side
        refs = [
            (disp.at[0, last, two], u0.at[0, shells, pair]),
            (layer.at[last, two], li.at[shells, pair]),
            (disp.at[0, last - 1, one], u0.at[0, shells - 1, edge]),
            (layer.at[last - 1, one], li.at[shells - 1, edge]),
            (force.at[0, last, one], fh.at[side[0]]),
        ]
        return [lateral(side, 0, a, b) for a, b in refs]

    def bulk_rest(side, i):
        s = order(i)
        return [lateral(side, 1 + i, disp.at[rest, s, side[4]], u0.at[rest, s + 1, side[6]])]

    def bulk_all(side, i):
        s = order(i)
        return [lateral(side, 1 + i, layer.at[s, side[4]], li.at[s + 1, side[6]]),
                lateral(side, 1 + i, disp.at[:, s, side[4]], u0.at[:, s + 1, side[6]])]

    def later_rest(side, i):
        s = order(i)
        return [lateral(side, 1 + shells + i, u1.at[rest, s + 1, side[8]], u1.at[rest, s + 1, side[6]])]

    def later_all(side, i):
        s = order(i)
        return [lateral(side, 1 + shells + i, u1.at[:, s + 1, side[8]], u1.at[:, s + 1, side[6]])]

    def for_shell(i, act, some, every):
        alone = jnp.logical_and(top, i < some[1])

        @pl.when(alone)
        def _():
            act(some[0])

        @pl.when(jnp.logical_not(alone))
        def _():
            act(every[0])

    odd = lax.rem(me, 2) == 1

    def nearer_first(go):
        @pl.when(odd)
        def _():
            go(sides[1])

        go(sides[0])

        @pl.when(jnp.logical_not(odd))
        def _():
            go(sides[1])

    def start_to(i, some, every):
        def go(side):
            @pl.when(side[1])
            def _():
                for_shell(i, lambda make: [c.start() for c in make(side, i)], some, every)

        nearer_first(go)

    def got_from(i, k, some, every):
        for side in sides:
            alone = jnp.logical_and(top, i < some[1])
            sem = x_recv.at[side[0], k + i]

            @pl.when(jnp.logical_and(side[2], alone))
            def _():
                arrived(span(some[2]), sem)

            @pl.when(jnp.logical_and(side[2], jnp.logical_not(alone)))
            def _():
                arrived(span(every[1]), sem)

    def span(count):
        parts = min(n for n in range(1, shells + 3) if count % n == 0 and count // n <= 8)
        return u0.at[0, pl.ds(0, parts), pl.ds(0, 8), pl.ds(0, count // parts * (lon // 8))]

    bulk = ((bulk_rest, 2, comps - 1), (bulk_all, comps + 1))
    later = ((later_rest, 1, comps - 1), (later_all, comps))
    rows_first = 7
    rows_top = rows_first + sum(k[0][1] * k[0][2] + (shells - k[0][1]) * k[1][1] for k in (bulk, later))
    rows_other = sum(shells * k[1][1] for k in (bulk, later))

    def across(k, source, target):
        return pltpu.make_async_remote_copy(
            src_ref=source, dst_ref=target, send_sem=send_sem.at[2 + k], recv_sem=r_recv.at[k],
            device_id={"radial": rad - 1 - place}, device_id_type=MESH)

    beyond = jnp.where(top, shells + 1, 0)
    facing = jnp.where(top, 0, shells + 1)
    r_layer = across(0, layer.at[face], li.at[beyond, inner])
    r_disp = across(0, disp.at[:, face], u0.at[:, beyond, inner])
    r_later = across(1, u1.at[:, face + 1, inner], u1.at[:, beyond, inner])

    pl.semaphore_wait(barrier, greeted(1) + rad - 1)

    @pl.when(top)
    def _():
        def go(side):
            @pl.when(side[1])
            def _():
                for copy in first(side):
                    copy.start()

        nearer_first(go)

    r_layer.start()
    r_disp.start()
    c_rest = [load(disp.at[rest], u0.at[rest, pl.ds(1, shells), inner], 4), load(force.at[rest], fv.at[rest], 5)]
    greet(far_sem.at[0], steps[0])

    c_visc.wait()
    values = [visc_s[i] * 0.5 for i in range(layers)]

    def lookup_at(s, where):
        he[s, where, :] = choose(li[s, where, :], values)

    def lookup(s):
        for r in range(0, rows, 8):
            lookup_at(s, pl.ds(PAD + r, 8))

    def lookup_step(i, carry):
        lookup(order(i) + 1)
        return carry

    c_layer.wait()
    lax.fori_loop(0, shells, lookup_step, 0)

    start_to(0, *bulk)
    if steps[1:]:
        pl.semaphore_wait(far_sem.at[0], greeted(steps[0]))
        greet(far_sem.at[1], steps[1])

    tables = [(trig, trig_v), (response, resp_v), (cosine, cosine_v), (mask, mask_v)]
    for copy in c_first:
        copy.wait()
    c_tables = [load(a, b, 6 + k) for k, (a, b) in enumerate(tables)]
    start_to(1, *bulk)

    chunk = lon // 4

    def beside(load, k):
        first, end = k * chunk, (k + 1) * chunk
        mid = load(slice(first, end))
        before = load(slice((first - 128) % lon, (first - 128) % lon + 128))
        after = load(slice(end % lon, end % lon + 128))
        left = pltpu.roll(jnp.concatenate([before, mid], axis=1), 1, 1)[:, 128:]
        right = pltpu.roll(jnp.concatenate([mid, after], axis=1), chunk + 127, 1)[:, :chunk]
        return mid, left, right

    def sweep(src, s, r, size, some, pushed, store):
        here, next_row, last_row = slice(r, r + size), slice(r + 1, r + size + 1), slice(r - 1, r + size - 1)
        for k in range(4):
            lanes = slice(k * chunk, (k + 1) * chunk)
            h, left, right = beside(lambda cols: he[s + 1, here, cols], k)
            ws = [
                h + he[s + 2, here, lanes],
                h + he[s, here, lanes],
                h + he[s + 1, next_row, lanes],
                h + he[s + 1, last_row, lanes],
                h + left,
                h + right,
            ]
            rate = 0.8 / (1.0 + (((ws[0] + ws[1]) + (ws[2] + ws[3])) + (ws[4] + ws[5])))
            for c in some:
                u, left, right = beside(lambda cols: src[c, s + 1, here, cols], k)
                total = pushed(c, lanes)
                total = total + ws[0] * src[c, s + 2, here, lanes]
                total = total + ws[1] * src[c, s, here, lanes]
                total = total + ws[2] * src[c, s + 1, next_row, lanes]
                total = total + ws[3] * src[c, s + 1, last_row, lanes]
                total = total + ws[4] * left
                total = total + ws[5] * right
                store(c, lanes, 0.2 * u + rate * total)

    def sweep1(s, r, some, size=8):
        def store(c, lanes, value):
            u1[c, s + 1, PAD + r:PAD + r + size, lanes] = value

        sweep(u0, s, PAD + r, size, some, lambda c, lanes: fv[c, s, r:r + size, lanes], store)

    def sweep2(s, r, some):
        def store(c, lanes, value):
            out[c, s, r:r + 8, lanes] = value

        sweep(u1, s, PAD + r, 8, some, lambda c, lanes: fv[c, s, r:r + 8, lanes], store)

    edge_rows = sorted({0, rows - 8})
    inner_rows = list(range(8, rows - 8, 8))
    all_comps, rest_comps = list(range(comps)), list(range(1, comps))

    def inner1(i, carry):
        s = order(i)
        for r in inner_rows:
            sweep1(s, r, all_comps)
        return carry

    def inner1_first(i, carry):
        for r in inner_rows:
            sweep1(last - i, r, [0])
        sweep1(last - i, 1, [0], 7)
        sweep1(last - i, rows - 8, [0], 7)
        return carry

    def inner1_rest(i, carry):
        for r in inner_rows:
            sweep1(last - i, r, rest_comps)
        return carry

    @pl.when(top)
    def _():
        lax.fori_loop(0, 2, inner1_first, 0)
        for r in inner_rows:
            sweep2(last, r, [0])

    @pl.when(jnp.logical_not(top))
    def _():
        for copy in c_rest:
            copy.wait()
        lax.fori_loop(0, last, inner1, 0)

    for i in range(2, shells):
        start_to(i, *bulk)

    for k, step in enumerate(steps):
        if k > 1:
            pl.semaphore_wait(far_sem.at[k - 1], greeted(steps[k - 1]))
            greet(far_sem.at[k], step)

    quarter = lon // 4
    modes = trig.shape[2] // 2
    wave = lax.broadcasted_iota(jnp.int32, (rows, modes), 1) & 3
    zero, one = jnp.zeros((rows, modes), f32), jnp.ones((rows, modes), f32)
    e1 = jnp.where(wave == 0, one, jnp.where(wave == 2, -one, zero))
    s1 = jnp.where(wave == 1, one, jnp.where(wave == 3, -one, zero))
    e2 = jnp.where((wave & 1) == 0, one, -one)
    half = width // rad
    forward = []
    for d, e in [(d, e) for d in reversed(range(lat)) for e in range(rad) if d or e != rad - 1]:
        forward.append((d, e, pltpu.make_async_remote_copy(
            src_ref=fsend.at[peer(d) * rad + e], dst_ref=frecv.at[me],
            send_sem=send_sem.at[4], recv_sem=all_recv.at[0],
            device_id={"lateral": peer(d), "radial": e}, device_id_type=MESH)))

    @pl.when(top)
    def _():
        for side in sides:
            @pl.when(side[2])
            def _():
                arrived(span(rows_first), x_recv.at[side[0], 0])
                lookup_at(shells, side[7])
                lookup_at(shells - 1, side[6])

        def early(i, carry):
            for r in (0, rows - 1):
                sweep1(last - i, r, [0], 1)
            return carry

        lax.fori_loop(0, 2, early, 0)
        for side, row in zip(sides, (PAD - 1, PAD + rows)):
            @pl.when(side[2])
            def _():
                def store(c, lanes, value):
                    u1[c, shells, row:row + 1, lanes] = value

                sweep(u0, last, row, 1, [0], lambda c, lanes: fh[side[0], :, lanes], store)

        for r in edge_rows:
            sweep2(last, r, [0])

    c_tables[0].wait()

    @pl.when(top)
    def _():
        x = jnp.concatenate([out[0, last, :, quarter * m:quarter * (m + 1)] for m in range(4)], axis=0)
        xh, xl = split(x)
        g = dot(jnp.concatenate([xh, xl], axis=0), trig_v[0])
        g = g[:4 * rows] + g[4 * rows:] + dot(xh, trig_v[1])
        gc = [g[rows * m:rows * (m + 1), :modes] for m in range(4)]
        gs = [g[rows * m:rows * (m + 1), modes:] for m in range(4)]
        fc = gc[0] + e2 * gc[2] + e1 * (gc[1] + gc[3]) - s1 * (gs[1] - gs[3])
        fs = gs[0] + e2 * gs[2] + e1 * (gs[1] + gs[3]) + s1 * (gc[1] - gc[3])
        fourier = jnp.concatenate([fc, fs], axis=1)
        for p in range(lat):
            cols = slice(p * width, (p + 1) * width)
            fsend[p * rad], fsend[p * rad + 1] = swap(fourier[:rows // 2, cols], fourier[rows // 2:, cols])

    pl.semaphore_wait(far_sem.at[len(steps) - 1], greeted(steps[-1]))

    @pl.when(top)
    def _():
        far_first([(d, copy) for d, _, copy in forward])
        frecv[me] = fsend[me * rad + rad - 1]

        for copy in c_rest:
            copy.wait()


    def main(i, carry):
        s = order(i)

        got_from(i, 1, *bulk)
        for side in sides:
            @pl.when(jnp.logical_and(side[2], jnp.logical_not(jnp.logical_and(top, i < 2))))
            def _():
                lookup_at(s + 1, side[6])

        for r in edge_rows:
            sweep1(s, r, all_comps)
        start_to(i, *later)
        return carry

    def inner2(i, carry):
        s = order(i)
        alone = jnp.logical_and(top, i == 0)

        @pl.when(alone)
        def _():
            for r in inner_rows:
                sweep2(s, r, rest_comps)

        @pl.when(jnp.logical_not(alone))
        def _():
            for r in inner_rows:
                sweep2(s, r, all_comps)

        return carry

    ahead = jnp.where(top, last, 2)
    lax.fori_loop(0, ahead, main, 0)
    arrived(u0.at[0, pl.ds(0, comps + 1), inner], r_recv.at[0])
    lookup(facing)
    @pl.when(top)
    def _():
        lax.fori_loop(0, 2, inner1_rest, 0)

    lax.fori_loop(jnp.where(top, 2, last), shells, inner1, 0)
    inner2(0, 0)

    for copy in c_tables[1:]:
        copy.wait()
    answer = resp_v[:, :half]
    for e in range(1, rad):
        answer = jnp.where(place == e, resp_v[:, e * half:(e + 1) * half], answer)
    resp_t[...] = answer.T

    @pl.when(top)
    def _():
        arrived(frecv.at[pl.ds(0, lat - 1)], all_recv.at[0])

    @pl.when(jnp.logical_not(top))
    def _():
        arrived(frecv, all_recv.at[0])

    packed = frecv[...].reshape(lat * rows // 2, width)
    spectrum = jnp.concatenate([packed, pltpu.roll(packed, half, 1)], axis=0)
    low = lax.broadcasted_iota(jnp.int32, spectrum.shape, 1) < half
    sh = spectrum.astype(bf16).astype(f32)
    both = jnp.where(low, sh, pltpu.roll(spectrum - sh, half, 1)).astype(bf16)
    down = (((0,), (0,)), ((), ()))
    coef = dot(both, cosine_v[0], down)
    coef = coef[:half] + coef[half:] + dot(both[:, :half], cosine_v[1], down)
    sh, sl = split(resp_t[...] * coef)
    nt = (((1,), (1,)), ((), ()))
    load_rows = dot(cosine_v[0], jnp.concatenate([sh, sl], axis=0), nt)
    load_rows = load_rows + pltpu.roll(load_rows, half, 1) + dot(cosine_v[1], jnp.concatenate([sh, sh], axis=0), nt)
    upper, lower = load_rows[:lat * rows // 2], load_rows[lat * rows // 2:]
    gsend[...] = jnp.where(low[:lat * rows // 2], upper, lower).reshape(lat, rows // 2, width)
    back = []
    for d, e in offsets:
        back.append((d, pltpu.make_async_remote_copy(
            src_ref=gsend.at[peer(d)], dst_ref=grecv.at[me * rad + place],
            send_sem=send_sem.at[5], recv_sem=all_recv.at[1],
            device_id=around(d, e), device_id_type=MESH)))
    far_first(back)
    grecv[me * rad + place] = gsend[me]
    coef_out[...] = coef

    def final(i, carry):
        s = order(i)
        alone = jnp.logical_and(top, i == 0)

        @pl.when(i == last)
        def _():
            r_later.wait_recv()
            inner2(i, 0)

        got_from(i, 1 + shells, *later)

        @pl.when(alone)
        def _():
            for r in edge_rows:
                sweep2(s, r, rest_comps)

        @pl.when(jnp.logical_not(alone))
        def _():
            for r in edge_rows:
                sweep2(s, r, all_comps)

        return carry

    lax.fori_loop(ahead, shells, main, 0)
    r_later.start()

    lax.fori_loop(1, last, inner2, 0)


    lax.fori_loop(0, shells, final, 0)

    blocks = lat * rad - 1

    @pl.when(top)
    def _():
        arrived(fsend.at[pl.ds(0, blocks)], send_sem.at[4])

    for side in sides:
        for who, count in ((top, rows_top), (jnp.logical_not(top), rows_other)):
            @pl.when(jnp.logical_and(who, side[1]))
            def _():
                arrived(span(count), send_sem.at[side[0]])

    arrived(u0.at[0, pl.ds(0, comps + 1), inner], send_sem.at[2])
    arrived(u0.at[:, 0, inner], send_sem.at[3])
    arrived(grecv.at[pl.ds(0, blocks)], send_sem.at[5])
    arrived(grecv.at[pl.ds(0, blocks)], all_recv.at[1])
    for p in range(lat):
        cols = slice(p * width, (p + 1) * width)
        gather[:rows // 2, cols], gather[rows // 2:, cols] = swap(grecv[p * rad], grecv[p * rad + 1])


def finish(out, coef, gather, trig, mask, out_h, coef_h, sea_h, sea, sem):
    rows, lon = mask.shape
    quarter, modes = lon // 4, trig.shape[2] // 2
    copies = [pltpu.make_async_copy(out, out_h, sem.at[0]), pltpu.make_async_copy(coef, coef_h, sem.at[1])]
    for copy in copies:
        copy.start()
    wave = lax.broadcasted_iota(jnp.int32, (rows, modes), 1) & 3
    zero, one = jnp.zeros((rows, modes), f32), jnp.ones((rows, modes), f32)
    e1 = jnp.where(wave == 0, one, jnp.where(wave == 2, -one, zero))
    s1 = jnp.where(wave == 1, one, jnp.where(wave == 3, -one, zero))
    e2 = jnp.where((wave & 1) == 0, one, -one)
    rc, rs = gather[:, :modes], gather[:, modes:]
    twisted = [
        (rc, rs),
        (e1 * rc + s1 * rs, e1 * rs - s1 * rc),
        (e2 * rc, e2 * rs),
        (e1 * rc - s1 * rs, e1 * rs + s1 * rc),
    ]
    a = jnp.concatenate([jnp.concatenate(pair, axis=1) for pair in twisted], axis=0)
    ah, al = split(a)
    nt = (((1,), (1,)), ((), ()))
    total = dot(jnp.concatenate([ah, al], axis=0), trig[0], nt)
    total = total[:4 * rows] + total[4 * rows:] + dot(ah, trig[1], nt)
    for m in range(4):
        cut = slice(quarter * m, quarter * (m + 1))
        sea[:, cut] = mask[:, cut].astype(f32) * total[rows * m:rows * (m + 1)]
        copies.append(pltpu.make_async_copy(sea.at[:, cut], sea_h.at[:, cut], sem.at[2 + m]))
        copies[-1].start()
    for copy in copies:
        copy.wait()


def shards(lat, rad, disp, force, visc, layer, response, mask):
    comps, shells, rows, lon = disp.shape
    width = response.shape[1]
    trig = np.stack(longitude_quarter(lon, MODES))
    cosine = np.stack(colatitude_table(lat * rows, MODES)).reshape(2, lat, 2, rows // 2, MODES)
    cosine = cosine.transpose(0, 2, 1, 3, 4).reshape(2, lat * rows, MODES)
    tables = [trig, cosine]
    hbm = pl.BlockSpec(memory_space=pltpu.HBM)
    vmem = pl.BlockSpec(memory_space=pltpu.VMEM)
    tall = rows + 2 * PAD
    field = pltpu.VMEM((comps, shells + 2, tall, lon), f32)
    half = width // rad
    block = pltpu.VMEM((lat, rows // 2, width), f32)
    blocks = pltpu.VMEM((lat * rad, rows // 2, width), f32)
    dma = pltpu.SemaphoreType.DMA
    spare = 4 * (disp.size + MODES * width // rad + 2 * rows * MODES + rows * lon) + 2 * trig.size + 65536
    out, coef, gather, trig_v, mask_v = pl.pallas_call(
        functools.partial(kernel, lat, rad, visc.shape[0]),
        out_shape=(
            pltpu.VMEM(disp.shape, f32),
            pltpu.VMEM((width // rad, MODES), f32),
            pltpu.VMEM((rows, 2 * MODES), f32),
            pltpu.VMEM(trig.shape, bf16),
            pltpu.VMEM(mask.shape, jnp.int32),
        ),
        in_specs=[hbm] * 8,
        out_specs=(vmem,) * 5,
        scratch_shapes=[
            field, field,
            pltpu.VMEM((comps, shells, rows, lon), f32),
            pltpu.VMEM((2, 1, lon), f32),
            pltpu.VMEM((shells + 2, tall, lon), jnp.int32),
            pltpu.VMEM((shells + 2, tall, lon), f32),
            blocks, block, block, blocks,
            pltpu.VMEM(response.shape, f32), pltpu.VMEM((half, MODES), f32),
            pltpu.VMEM(cosine.shape, bf16),
            pltpu.SMEM(visc.shape, f32),
            dma((10,)), dma((6,)), dma((2, 1 + 2 * shells)), dma((2,)), dma((2,)),
            pltpu.SemaphoreType.REGULAR((max(1, (lat - 1).bit_length()),)),
        ],
        compiler_params=pltpu.CompilerParams(
            collective_id=0, has_side_effects=True, vmem_limit_bytes=VMEM - spare),
    )(disp, force, visc, layer, response, mask, *[jnp.asarray(t) for t in tables])
    out, coef, sea = pl.pallas_call(
        finish,
        out_shape=tuple(jax.ShapeDtypeStruct(shape, f32) for shape in (out.shape, coef.shape, mask.shape)),
        in_specs=[vmem] * 5,
        out_specs=(hbm, hbm, hbm),
        scratch_shapes=[pltpu.VMEM(mask.shape, f32), dma((6,))],
        compiler_params=pltpu.CompilerParams(vmem_limit_bytes=8 << 20),
    )(out, coef, gather, trig_v, mask_v)
    return out, coef.T, sea


def solution(mesh):
    in_specs = (
        P("member", "radial", "lateral", None),
        P("member", "radial", "lateral", None),
        P("member"),
        P("radial", "lateral", None),
        P(None, "lateral"),
        P("lateral", None),
    )
    out_specs = (
        P("member", "radial", "lateral", None),
        P("member", ("lateral", "radial")),
        P("lateral", "member"),
    )
    body = functools.partial(shards, mesh.shape["lateral"], mesh.shape["radial"])
    return jax.shard_map(body, mesh=mesh, in_specs=in_specs, out_specs=out_specs, check_vma=False)
```

```python
import functools
import math

import jax
import jax.numpy as jnp
import ml_dtypes
import numpy as np
from jax import lax
from jax.experimental import pallas as pl
from jax.experimental.pallas import tpu as pltpu
from jax.sharding import PartitionSpec as P

MODES = 512
PAD = 8
VMEM = 67043328
MESH = pl.DeviceIdType.MESH
f32, bf16 = jnp.float32, jnp.bfloat16


def halves(table):
    table = table.astype(np.float32)
    high = table.astype(ml_dtypes.bfloat16)
    low = (table - high.astype(np.float32)).astype(ml_dtypes.bfloat16)
    return high, low


def longitude_quarter(count, modes):
    points = np.arange(count // 4)[:, None]
    phase = points * np.arange(modes)[None, :] % count
    angle = 2.0 * math.pi / count * phase
    table = np.concatenate([np.cos(angle), np.sin(angle)], axis=1)
    return halves(table * math.sqrt(2.0 / count))


def colatitude_table(count, modes):
    points = np.arange(count)[:, None]
    phase = np.arange(modes)[None, :] * (2 * points + 1) % (4 * count)
    table = np.cos(math.pi / (2 * count) * phase) * math.sqrt(2.0 / count)
    return halves(table)


def split(x):
    high = x.astype(bf16)
    return high, (x - high.astype(f32)).astype(bf16)


def dot(a, b, dims=(((1,), (0,)), ((), ()))):
    return lax.dot_general(a, b, dims, preferred_element_type=f32)


def swap(a, b):
    half = a.shape[-1] // 2
    low = lax.broadcasted_iota(jnp.int32, a.shape, a.ndim - 1) < half
    return jnp.where(low, a, pltpu.roll(b, half, a.ndim - 1)), jnp.where(low, pltpu.roll(a, half, a.ndim - 1), b)


def choose(index, values):
    bit = 0
    while len(values) > 1:
        odd = (index & (1 << bit)) != 0
        values = [
            jnp.where(odd, values[min(i + 1, len(values) - 1)], values[i])
            for i in range(0, len(values), 2)
        ]
        bit += 1
    return values[0]


def kernel(lat, rad, layers, disp, force, visc, layer, response, mask, trig, cosine,
           out, coef_out, gather, trig_v, mask_v,
           u0, u1, fv, fh, li, he, fsend, frecv, gsend, grecv, resp_v, resp_t, cosine_v, visc_s,
           load_sem, send_sem, x_recv, r_recv, all_recv, far_sem):
    comps, shells, rows, lon = disp.shape
    width = response.shape[1]
    me = lax.axis_index("lateral")
    place = lax.axis_index("radial")
    inner = pl.ds(PAD, rows)
    last = shells - 1
    top = place == rad - 1
    south, north = me < lat - 1, me > 0
    face = jnp.where(top, 0, last)

    def order(i):
        return jnp.where(top, last - i, i)

    def load(source, target, index):
        copy = pltpu.make_async_copy(source, target, load_sem.at[index])
        copy.start()
        return copy

    def arrived(ref, sem):
        pltpu.make_async_copy(ref, ref, sem).wait()

    def peer(d):
        return me ^ d if lat & (lat - 1) == 0 else lax.rem(me + d, lat)

    def around(d, e):
        return {"lateral": peer(d), "radial": lax.rem(place + e, rad)}

    offsets = [(d, e) for d in reversed(range(lat)) for e in range(rad) if d or e]
    quarters = max(1, lat // 4)
    middle = jnp.logical_and(me >= quarters, me < lat - quarters)

    def far_first(copies):
        for here, rank in ((middle, [2, 3, 1, 0]), (jnp.logical_not(middle), [3, 2, 1, 0])):
            @pl.when(here)
            def _():
                for _, copy in sorted(copies, key=lambda pair: rank.index(min(3, pair[0] // quarters))):
                    copy.start()

    barrier = pltpu.get_barrier_semaphore()
    for e in range(1, rad):
        pl.semaphore_signal(barrier, inc=1, device_id=around(0, e), device_id_type=MESH)

    def greet(sem, step):
        @pl.when(me + step < lat)
        def _():
            pl.semaphore_signal(sem, inc=1, device_id={"lateral": me + step}, device_id_type=MESH)

        @pl.when(me >= step)
        def _():
            pl.semaphore_signal(sem, inc=1, device_id={"lateral": me - step}, device_id_type=MESH)

    def greeted(step):
        return jnp.where(me + step < lat, 1, 0) + jnp.where(me >= step, 1, 0)

    greet(barrier, 1)
    steps = [1 << k for k in range((lat - 1).bit_length())]

    c_visc = load(visc, visc_s, 0)
    c_layer = load(layer, li.at[pl.ds(1, shells), inner], 1)
    rest = pl.ds(1, comps - 1)
    c_first = [load(disp.at[0], u0.at[0, pl.ds(1, shells), inner], 2), load(force.at[0], fv.at[0], 3)]

    void = jnp.where(top, shells + 1, 0)
    tall, wide = rows + 2 * PAD, (1, lon)
    he[void] = jnp.zeros((tall, lon), f32)
    for c in range(comps):
        u0[c, void] = jnp.zeros((tall, lon), f32)
        u1[c, void] = jnp.zeros((tall, lon), f32)

    def unpadded(row):
        for s in range(1, shells + 1):
            he[s, row:row + 1, :] = jnp.zeros(wide, f32)
            for c in range(comps):
                u0[c, s, row:row + 1, :] = jnp.zeros(wide, f32)
                u1[c, s, row:row + 1, :] = jnp.zeros(wide, f32)

    @pl.when(jnp.logical_not(north))
    def _():
        unpadded(PAD - 1)

    @pl.when(jnp.logical_not(south))
    def _():
        unpadded(PAD + rows)

    sides = [
        (0, south, north, jnp.where(south, me + 1, me), pl.ds(rows - 1, 1), pl.ds(rows - 2, 2),
         pl.ds(PAD - 1, 1), pl.ds(PAD - 2, 2), pl.ds(PAD + rows - 1, 1)),
        (1, north, south, jnp.where(north, me - 1, me), pl.ds(0, 1), pl.ds(0, 2),
         pl.ds(PAD + rows, 1), pl.ds(PAD + rows, 2), pl.ds(PAD, 1)),
    ]

    def lateral(side, k, source, target):
        return pltpu.make_async_remote_copy(
            src_ref=source, dst_ref=target, send_sem=send_sem.at[side[0]], recv_sem=x_recv.at[side[0], k],
            device_id={"lateral": side[3]}, device_id_type=MESH)

    def first(side):
        _, _, _, _, one, two, edge, pair, _ = side
        refs = [
            (disp.at[0, last, two], u0.at[0, shells, pair]),
            (layer.at[last, two], li.at[shells, pair]),
            (disp.at[0, last - 1, one], u0.at[0, shells - 1, edge]),
            (layer.at[last - 1, one], li.at[shells - 1, edge]),
            (force.at[0, last, one], fh.at[side[0]]),
        ]
        return [lateral(side, 0, a, b) for a, b in refs]

    def bulk_rest(side, i):
        s = order(i)
        return [lateral(side, 1 + i, disp.at[rest, s, side[4]], u0.at[rest, s + 1, side[6]])]

    def bulk_all(side, i):
        s = order(i)
        return [lateral(side, 1 + i, layer.at[s, side[4]], li.at[s + 1, side[6]]),
                lateral(side, 1 + i, disp.at[:, s, side[4]], u0.at[:, s + 1, side[6]])]

    def later_rest(side, i):
        s = order(i)
        return [lateral(side, 1 + shells + i, u1.at[rest, s + 1, side[8]], u1.at[rest, s + 1, side[6]])]

    def later_all(side, i):
        s = order(i)
        return [lateral(side, 1 + shells + i, u1.at[:, s + 1, side[8]], u1.at[:, s + 1, side[6]])]

    def for_shell(i, act, some, every):
        alone = jnp.logical_and(top, i < some[1])

        @pl.when(alone)
        def _():
            act(some[0])

        @pl.when(jnp.logical_not(alone))
        def _():
            act(every[0])

    odd = lax.rem(me, 2) == 1

    def nearer_first(go):
        @pl.when(odd)
        def _():
            go(sides[1])

        go(sides[0])

        @pl.when(jnp.logical_not(odd))
        def _():
            go(sides[1])

    def start_to(i, some, every):
        def go(side):
            @pl.when(side[1])
            def _():
                for_shell(i, lambda make: [c.start() for c in make(side, i)], some, every)

        nearer_first(go)

    def got_from(i, k, some, every):
        for side in sides:
            alone = jnp.logical_and(top, i < some[1])
            sem = x_recv.at[side[0], k + i]

            @pl.when(jnp.logical_and(side[2], alone))
            def _():
                arrived(span(some[2]), sem)

            @pl.when(jnp.logical_and(side[2], jnp.logical_not(alone)))
            def _():
                arrived(span(every[1]), sem)

    def span(count):
        parts = min(n for n in range(1, shells + 3) if count % n == 0 and count // n <= 8)
        return u0.at[0, pl.ds(0, parts), pl.ds(0, 8), pl.ds(0, count // parts * (lon // 8))]

    bulk = ((bulk_rest, 2, comps - 1), (bulk_all, comps + 1))
    later = ((later_rest, 1, comps - 1), (later_all, comps))
    rows_first = 7
    rows_top = rows_first + sum(k[0][1] * k[0][2] + (shells - k[0][1]) * k[1][1] for k in (bulk, later))
    rows_other = sum(shells * k[1][1] for k in (bulk, later))

    def across(k, source, target):
        return pltpu.make_async_remote_copy(
            src_ref=source, dst_ref=target, send_sem=send_sem.at[2 + k], recv_sem=r_recv.at[k],
            device_id={"radial": rad - 1 - place}, device_id_type=MESH)

    beyond = jnp.where(top, shells + 1, 0)
    facing = jnp.where(top, 0, shells + 1)
    r_layer = across(0, layer.at[face], li.at[beyond, inner])
    r_disp = across(0, disp.at[:, face], u0.at[:, beyond, inner])
    r_later = across(1, u1.at[:, face + 1, inner], u1.at[:, beyond, inner])

    pl.semaphore_wait(barrier, greeted(1) + rad - 1)

    @pl.when(top)
    def _():
        def go(side):
            @pl.when(side[1])
            def _():
                for copy in first(side):
                    copy.start()

        nearer_first(go)

    r_layer.start()
    r_disp.start()
    c_rest = [load(disp.at[rest], u0.at[rest, pl.ds(1, shells), inner], 4), load(force.at[rest], fv.at[rest], 5)]
    greet(far_sem.at[0], steps[0])

    c_visc.wait()
    values = [visc_s[i] * 0.5 for i in range(layers)]

    def lookup_at(s, where):
        he[s, where, :] = choose(li[s, where, :], values)

    def lookup(s):
        for r in range(0, rows, 8):
            lookup_at(s, pl.ds(PAD + r, 8))

    def lookup_step(i, carry):
        lookup(order(i) + 1)
        return carry

    c_layer.wait()
    lax.fori_loop(0, shells, lookup_step, 0)

    start_to(0, *bulk)
    if steps[1:]:
        pl.semaphore_wait(far_sem.at[0], greeted(steps[0]))
        greet(far_sem.at[1], steps[1])

    tables = [(response, resp_v), (trig, trig_v), (cosine, cosine_v), (mask, mask_v)]
    for copy in c_first:
        copy.wait()
    c_tables = [load(a, b, 6 + k) for k, (a, b) in enumerate(tables)]
    start_to(1, *bulk)

    chunk = lon // 4

    def beside(load, k):
        first, end = k * chunk, (k + 1) * chunk
        mid = load(slice(first, end))
        before = load(slice((first - 128) % lon, (first - 128) % lon + 128))
        after = load(slice(end % lon, end % lon + 128))
        left = pltpu.roll(jnp.concatenate([before, mid], axis=1), 1, 1)[:, 128:]
        right = pltpu.roll(jnp.concatenate([mid, after], axis=1), chunk + 127, 1)[:, :chunk]
        return mid, left, right

    def sweep(src, s, r, size, some, pushed, store):
        here, next_row, last_row = slice(r, r + size), slice(r + 1, r + size + 1), slice(r - 1, r + size - 1)
        for k in range(4):
            lanes = slice(k * chunk, (k + 1) * chunk)
            h, left, right = beside(lambda cols: he[s + 1, here, cols], k)
            ws = [
                h + he[s + 2, here, lanes],
                h + he[s, here, lanes],
                h + he[s + 1, next_row, lanes],
                h + he[s + 1, last_row, lanes],
                h + left,
                h + right,
            ]
            rate = 0.8 / (1.0 + (((ws[0] + ws[1]) + (ws[2] + ws[3])) + (ws[4] + ws[5])))
            for c in some:
                u, left, right = beside(lambda cols: src[c, s + 1, here, cols], k)
                total = pushed(c, lanes)
                total = total + ws[0] * src[c, s + 2, here, lanes]
                total = total + ws[1] * src[c, s, here, lanes]
                total = total + ws[2] * src[c, s + 1, next_row, lanes]
                total = total + ws[3] * src[c, s + 1, last_row, lanes]
                total = total + ws[4] * left
                total = total + ws[5] * right
                store(c, lanes, 0.2 * u + rate * total)

    def sweep1(s, r, some, size=8):
        def store(c, lanes, value):
            u1[c, s + 1, PAD + r:PAD + r + size, lanes] = value

        sweep(u0, s, PAD + r, size, some, lambda c, lanes: fv[c, s, r:r + size, lanes], store)

    def sweep2(s, r, some):
        def store(c, lanes, value):
            out[c, s, r:r + 8, lanes] = value

        sweep(u1, s, PAD + r, 8, some, lambda c, lanes: fv[c, s, r:r + 8, lanes], store)

    edge_rows = sorted({0, rows - 8})
    inner_rows = list(range(8, rows - 8, 8))
    all_comps, rest_comps = list(range(comps)), list(range(1, comps))

    def inner1(i, carry):
        s = order(i)
        for r in inner_rows:
            sweep1(s, r, all_comps)
        return carry

    def inner1_first(i, carry):
        for r in inner_rows:
            sweep1(last - i, r, [0])
        sweep1(last - i, 1, [0], 7)
        sweep1(last - i, rows - 8, [0], 7)
        return carry

    def inner1_rest(i, carry):
        for r in inner_rows:
            sweep1(last - i, r, rest_comps)
        return carry

    @pl.when(top)
    def _():
        lax.fori_loop(0, 2, inner1_first, 0)
        for r in inner_rows:
            sweep2(last, r, [0])

    @pl.when(jnp.logical_not(top))
    def _():
        for copy in c_rest:
            copy.wait()
        lax.fori_loop(0, last, inner1, 0)

    for i in range(2, shells):
        start_to(i, *bulk)

    for k, step in enumerate(steps):
        if k > 1:
            pl.semaphore_wait(far_sem.at[k - 1], greeted(steps[k - 1]))
            greet(far_sem.at[k], step)

    quarter = lon // 4
    modes = trig.shape[2] // 2
    wave = lax.broadcasted_iota(jnp.int32, (rows, modes), 1) & 3
    zero, one = jnp.zeros((rows, modes), f32), jnp.ones((rows, modes), f32)
    e1 = jnp.where(wave == 0, one, jnp.where(wave == 2, -one, zero))
    s1 = jnp.where(wave == 1, one, jnp.where(wave == 3, -one, zero))
    e2 = jnp.where((wave & 1) == 0, one, -one)
    half = width // rad
    forward = []
    for d, e in [(d, e) for d in reversed(range(lat)) for e in range(rad) if d or e != rad - 1]:
        forward.append((d, e, pltpu.make_async_remote_copy(
            src_ref=fsend.at[peer(d) * rad + e], dst_ref=frecv.at[me],
            send_sem=send_sem.at[4], recv_sem=all_recv.at[0],
            device_id={"lateral": peer(d), "radial": e}, device_id_type=MESH)))

    c_tables[0].wait()
    answer = resp_v[:, :half]
    for e in range(1, rad):
        answer = jnp.where(place == e, resp_v[:, e * half:(e + 1) * half], answer)
    resp_t[...] = answer.T

    @pl.when(top)
    def _():
        for side in sides:
            @pl.when(side[2])
            def _():
                arrived(span(rows_first), x_recv.at[side[0], 0])
                lookup_at(shells, side[7])
                lookup_at(shells - 1, side[6])

        def early(i, carry):
            for r in (0, rows - 1):
                sweep1(last - i, r, [0], 1)
            return carry

        lax.fori_loop(0, 2, early, 0)
        for side, row in zip(sides, (PAD - 1, PAD + rows)):
            @pl.when(side[2])
            def _():
                def store(c, lanes, value):
                    u1[c, shells, row:row + 1, lanes] = value

                sweep(u0, last, row, 1, [0], lambda c, lanes: fh[side[0], :, lanes], store)

        for r in edge_rows:
            sweep2(last, r, [0])

    c_tables[1].wait()

    @pl.when(top)
    def _():
        x = jnp.concatenate([out[0, last, :, quarter * m:quarter * (m + 1)] for m in range(4)], axis=0)
        xh, xl = split(x)
        g = dot(jnp.concatenate([xh, xl], axis=0), trig_v[0])
        g = g[:4 * rows] + g[4 * rows:] + dot(xh, trig_v[1])
        gc = [g[rows * m:rows * (m + 1), :modes] for m in range(4)]
        gs = [g[rows * m:rows * (m + 1), modes:] for m in range(4)]
        fc = gc[0] + e2 * gc[2] + e1 * (gc[1] + gc[3]) - s1 * (gs[1] - gs[3])
        fs = gs[0] + e2 * gs[2] + e1 * (gs[1] + gs[3]) + s1 * (gc[1] - gc[3])
        fourier = jnp.concatenate([fc, fs], axis=1)
        for p in range(lat):
            cols = slice(p * width, (p + 1) * width)
            fsend[p * rad], fsend[p * rad + 1] = swap(fourier[:rows // 2, cols], fourier[rows // 2:, cols])

    pl.semaphore_wait(far_sem.at[len(steps) - 1], greeted(steps[-1]))

    @pl.when(top)
    def _():
        far_first([(d, copy) for d, _, copy in forward])
        frecv[me] = fsend[me * rad + rad - 1]

        for copy in c_rest:
            copy.wait()


    def main(i, carry):
        s = order(i)

        got_from(i, 1, *bulk)
        for side in sides:
            @pl.when(jnp.logical_and(side[2], jnp.logical_not(jnp.logical_and(top, i < 2))))
            def _():
                lookup_at(s + 1, side[6])

        for r in edge_rows:
            sweep1(s, r, all_comps)
        start_to(i, *later)
        return carry

    def inner2(i, carry):
        s = order(i)
        alone = jnp.logical_and(top, i == 0)

        @pl.when(alone)
        def _():
            for r in inner_rows:
                sweep2(s, r, rest_comps)

        @pl.when(jnp.logical_not(alone))
        def _():
            for r in inner_rows:
                sweep2(s, r, all_comps)

        return carry

    ahead = jnp.where(top, last, 2)
    lax.fori_loop(0, ahead, main, 0)
    arrived(u0.at[0, pl.ds(0, comps + 1), inner], r_recv.at[0])
    lookup(facing)
    @pl.when(top)
    def _():
        lax.fori_loop(0, 2, inner1_rest, 0)

    lax.fori_loop(jnp.where(top, 2, last), shells, inner1, 0)
    inner2(0, 0)

    for copy in c_tables[2:]:
        copy.wait()

    @pl.when(top)
    def _():
        arrived(frecv.at[pl.ds(0, lat - 1)], all_recv.at[0])

    @pl.when(jnp.logical_not(top))
    def _():
        arrived(frecv, all_recv.at[0])

    packed = frecv[...].reshape(lat * rows // 2, width)
    spectrum = jnp.concatenate([packed, pltpu.roll(packed, half, 1)], axis=0)
    low = lax.broadcasted_iota(jnp.int32, spectrum.shape, 1) < half
    sh = spectrum.astype(bf16).astype(f32)
    both = jnp.where(low, sh, pltpu.roll(spectrum - sh, half, 1)).astype(bf16)
    down = (((0,), (0,)), ((), ()))
    coef = dot(both, cosine_v[0], down)
    coef = coef[:half] + coef[half:] + dot(both[:, :half], cosine_v[1], down)
    sh, sl = split(resp_t[...] * coef)
    nt = (((1,), (1,)), ((), ()))
    load_rows = dot(cosine_v[0], jnp.concatenate([sh, sl], axis=0), nt)
    load_rows = load_rows + pltpu.roll(load_rows, half, 1) + dot(cosine_v[1], jnp.concatenate([sh, sh], axis=0), nt)
    upper, lower = load_rows[:lat * rows // 2], load_rows[lat * rows // 2:]
    gsend[...] = jnp.where(low[:lat * rows // 2], upper, lower).reshape(lat, rows // 2, width)
    back = []
    for d, e in offsets:
        back.append((d, pltpu.make_async_remote_copy(
            src_ref=gsend.at[peer(d)], dst_ref=grecv.at[me * rad + place],
            send_sem=send_sem.at[5], recv_sem=all_recv.at[1],
            device_id=around(d, e), device_id_type=MESH)))
    far_first(back)
    grecv[me * rad + place] = gsend[me]
    coef_out[...] = coef

    def final(i, carry):
        s = order(i)
        alone = jnp.logical_and(top, i == 0)

        @pl.when(i == last)
        def _():
            r_later.wait_recv()
            inner2(i, 0)

        got_from(i, 1 + shells, *later)

        @pl.when(alone)
        def _():
            for r in edge_rows:
                sweep2(s, r, rest_comps)

        @pl.when(jnp.logical_not(alone))
        def _():
            for r in edge_rows:
                sweep2(s, r, all_comps)

        return carry

    lax.fori_loop(ahead, shells, main, 0)
    r_later.start()

    lax.fori_loop(1, last, inner2, 0)


    lax.fori_loop(0, shells, final, 0)

    blocks = lat * rad - 1

    @pl.when(top)
    def _():
        arrived(fsend.at[pl.ds(0, blocks)], send_sem.at[4])

    for side in sides:
        for who, count in ((top, rows_top), (jnp.logical_not(top), rows_other)):
            @pl.when(jnp.logical_and(who, side[1]))
            def _():
                arrived(span(count), send_sem.at[side[0]])

    arrived(u0.at[0, pl.ds(0, comps + 1), inner], send_sem.at[2])
    arrived(u0.at[:, 0, inner], send_sem.at[3])
    arrived(grecv.at[pl.ds(0, blocks)], send_sem.at[5])
    arrived(grecv.at[pl.ds(0, blocks)], all_recv.at[1])
    for p in range(lat):
        cols = slice(p * width, (p + 1) * width)
        gather[:rows // 2, cols], gather[rows // 2:, cols] = swap(grecv[p * rad], grecv[p * rad + 1])


def finish(out, coef, gather, trig, mask, out_h, coef_h, sea_h, sea, sem):
    rows, lon = mask.shape
    quarter, modes = lon // 4, trig.shape[2] // 2
    copies = [pltpu.make_async_copy(out, out_h, sem.at[0]), pltpu.make_async_copy(coef, coef_h, sem.at[1])]
    for copy in copies:
        copy.start()
    wave = lax.broadcasted_iota(jnp.int32, (rows, modes), 1) & 3
    zero, one = jnp.zeros((rows, modes), f32), jnp.ones((rows, modes), f32)
    e1 = jnp.where(wave == 0, one, jnp.where(wave == 2, -one, zero))
    s1 = jnp.where(wave == 1, one, jnp.where(wave == 3, -one, zero))
    e2 = jnp.where((wave & 1) == 0, one, -one)
    rc, rs = gather[:, :modes], gather[:, modes:]
    twisted = [
        (rc, rs),
        (e1 * rc + s1 * rs, e1 * rs - s1 * rc),
        (e2 * rc, e2 * rs),
        (e1 * rc - s1 * rs, e1 * rs + s1 * rc),
    ]
    a = jnp.concatenate([jnp.concatenate(pair, axis=1) for pair in twisted], axis=0)
    ah, al = split(a)
    nt = (((1,), (1,)), ((), ()))
    total = dot(jnp.concatenate([ah, al], axis=0), trig[0], nt)
    total = total[:4 * rows] + total[4 * rows:] + dot(ah, trig[1], nt)
    for m in range(4):
        cut = slice(quarter * m, quarter * (m + 1))
        sea[:, cut] = mask[:, cut].astype(f32) * total[rows * m:rows * (m + 1)]
        copies.append(pltpu.make_async_copy(sea.at[:, cut], sea_h.at[:, cut], sem.at[2 + m]))
        copies[-1].start()
    for copy in copies:
        copy.wait()


def shards(lat, rad, disp, force, visc, layer, response, mask):
    comps, shells, rows, lon = disp.shape
    width = response.shape[1]
    trig = np.stack(longitude_quarter(lon, MODES))
    cosine = np.stack(colatitude_table(lat * rows, MODES)).reshape(2, lat, 2, rows // 2, MODES)
    cosine = cosine.transpose(0, 2, 1, 3, 4).reshape(2, lat * rows, MODES)
    tables = [trig, cosine]
    hbm = pl.BlockSpec(memory_space=pltpu.HBM)
    vmem = pl.BlockSpec(memory_space=pltpu.VMEM)
    tall = rows + 2 * PAD
    field = pltpu.VMEM((comps, shells + 2, tall, lon), f32)
    half = width // rad
    block = pltpu.VMEM((lat, rows // 2, width), f32)
    blocks = pltpu.VMEM((lat * rad, rows // 2, width), f32)
    dma = pltpu.SemaphoreType.DMA
    spare = 4 * (disp.size + MODES * width // rad + 2 * rows * MODES + rows * lon) + 2 * trig.size + 65536
    out, coef, gather, trig_v, mask_v = pl.pallas_call(
        functools.partial(kernel, lat, rad, visc.shape[0]),
        out_shape=(
            pltpu.VMEM(disp.shape, f32),
            pltpu.VMEM((width // rad, MODES), f32),
            pltpu.VMEM((rows, 2 * MODES), f32),
            pltpu.VMEM(trig.shape, bf16),
            pltpu.VMEM(mask.shape, jnp.int32),
        ),
        in_specs=[hbm] * 8,
        out_specs=(vmem,) * 5,
        scratch_shapes=[
            field, field,
            pltpu.VMEM((comps, shells, rows, lon), f32),
            pltpu.VMEM((2, 1, lon), f32),
            pltpu.VMEM((shells + 2, tall, lon), jnp.int32),
            pltpu.VMEM((shells + 2, tall, lon), f32),
            blocks, block, block, blocks,
            pltpu.VMEM(response.shape, f32), pltpu.VMEM((half, MODES), f32),
            pltpu.VMEM(cosine.shape, bf16),
            pltpu.SMEM(visc.shape, f32),
            dma((10,)), dma((6,)), dma((2, 1 + 2 * shells)), dma((2,)), dma((2,)),
            pltpu.SemaphoreType.REGULAR((max(1, (lat - 1).bit_length()),)),
        ],
        compiler_params=pltpu.CompilerParams(
            collective_id=0, has_side_effects=True, vmem_limit_bytes=VMEM - spare),
    )(disp, force, visc, layer, response, mask, *[jnp.asarray(t) for t in tables])
    out, coef, sea = pl.pallas_call(
        finish,
        out_shape=tuple(jax.ShapeDtypeStruct(shape, f32) for shape in (out.shape, coef.shape, mask.shape)),
        in_specs=[vmem] * 5,
        out_specs=(hbm, hbm, hbm),
        scratch_shapes=[pltpu.VMEM(mask.shape, f32), dma((6,))],
        compiler_params=pltpu.CompilerParams(vmem_limit_bytes=8 << 20),
    )(out, coef, gather, trig_v, mask_v)
    return out, coef.T, sea


def solution(mesh):
    in_specs = (
        P("member", "radial", "lateral", None),
        P("member", "radial", "lateral", None),
        P("member"),
        P("radial", "lateral", None),
        P(None, "lateral"),
        P("lateral", None),
    )
    out_specs = (
        P("member", "radial", "lateral", None),
        P("member", ("lateral", "radial")),
        P("lateral", "member"),
    )
    body = functools.partial(shards, mesh.shape["lateral"], mesh.shape["radial"])
    return jax.shard_map(body, mesh=mesh, in_specs=in_specs, out_specs=out_specs, check_vma=False)
```
